128 devices in a mesh: row: 8 (over x, core), col: 16 (over z, y).
Axes of the slice: x: 4, y: 4, z: 4, core: 2. Of those that a mesh axis runs over, the one named last changes fastest.
Arguments:
- sdf_grids: bfloat16 [65536, 4096], P(('row', 'col')), may hold values from -6 to 6
- grain_poses: float32 [12, 65536], P(None, ('row', 'col')), may hold values from -4 to 4
- surface_nodes: float32 [65536, 768], P(('row', 'col')), may hold values from -5 to 5
- send_list: int32 [8, 16, 8, 32], P('row', 'col'), may hold values from 0 to 511, as said below
- pair_first: int32 [16384], P(('row', 'col')), may hold values from 0 to 511
- pair_sdf: int32 [16384], P(('row', 'col')), may hold values from 0 to 767, as said below
- pair_pose: int32 [16384], P(('row', 'col')), may hold values from 0 to 4607, as said below
- pair_live: int32 [16384], P(('row', 'col')), may hold values from 0 to 1, as said below
- knot_cells: int32 [16384, 768], P(('row', 'col')), may hold values from 1 to 13
- offsets: float32 [16384, 768], P(('row', 'col')), may hold values from 0 to 1
Outputs:
- grain_loads: float32 [6, 65536], P(None, ('row', 'col'))
The draws below stay inside these ranges and needn't reach their ends.
Inputs may be any that keep to these rules, and one draw needn't show every extreme that they name: `send_list`: the 8 lists of one device name distinct own grains each; list d is meant for the neighbour at offset d of the direction order; the neighbour's pairs name only slots of list d below a count from 8 to 32; on every device one of its 8 lists has count 32. `pair_sdf`: below 512: an own grain other than the first grain. From 512 on: ghost block d and slot s of an existing neighbour. `pair_pose`: names the pose of the same grain as pair_sdf: an own grain in the centre block, or the neighbour's listed grain. `pair_live`: on each device the live slots come first; their number is 128 divided by 1, 2 or 4, and some device has all slots live.
All inputs are finite; a program needn't handle non-finite values.
Results may differ from the reference program's by a relative error of at most 0.0057.
Values may be sent and summed in bfloat16 or wider, within the bound.
No kernel may reach another device: no remote copies, remote signals or barrier semaphores. Data moves between devices by JAX's collectives and lax.ppermute only.
A program may use at most 64 MiB of HBM per device.

```python
import jax
import jax.numpy as jnp
from jax import lax

GRID = 16
NODES = 256
GR_DEV = 512
GHOST = 32
PAIRS_DEV = 128
GRAINS = 65536
PAIRS = 16384
N_ROW = 8
N_COL = 16


DIRECTIONS = ((-1, -1), (-1, 0), (-1, 1), (0, -1), (0, 1), (1, -1), (1, 0), (1, 1))


def layout(key):
    devices = N_ROW * N_COL
    key_list = jax.random.split(jax.random.fold_in(key, 101), devices * 8)
    listed = jax.vmap(lambda single: jax.random.permutation(single, GR_DEV)[:GHOST])(key_list)
    listed = listed.astype(jnp.int32).reshape(N_ROW, N_COL, 8, GHOST)
    counts = jax.random.randint(jax.random.fold_in(key, 102), (N_ROW, N_COL, 8), max(1, GHOST // 4), GHOST + 1)
    full_dir = jax.random.randint(jax.random.fold_in(key, 103), (N_ROW, N_COL, 1), 0, 8)
    counts = jnp.where(jnp.arange(8, dtype=jnp.int32)[None, None, :] == full_dir, GHOST, counts)
    grid_shape = (N_ROW, N_COL, PAIRS_DEV)
    owner_grain = jax.random.randint(jax.random.fold_in(key, 104), grid_shape, 0, GR_DEV)
    partner = (owner_grain + 1 + jax.random.randint(jax.random.fold_in(key, 105), grid_shape, 0, GR_DEV - 1)) % GR_DEV
    wanted = jax.random.randint(jax.random.fold_in(key, 106), grid_shape, 0, 2)
    direction = jax.random.randint(jax.random.fold_in(key, 107), grid_shape, 0, 8)
    raw_slot = jax.random.randint(jax.random.fold_in(key, 108), grid_shape, 0, GHOST)
    step_table = jnp.array(DIRECTIONS, dtype=jnp.int32)
    row_at = jnp.arange(N_ROW, dtype=jnp.int32)[:, None, None] + step_table[direction, 0]
    col_at = jnp.arange(N_COL, dtype=jnp.int32)[None, :, None] + step_table[direction, 1]
    inside = (row_at >= 0) & (row_at < N_ROW) & (col_at >= 0) & (col_at < N_COL)
    row_at = jnp.clip(row_at, 0, N_ROW - 1)
    col_at = jnp.clip(col_at, 0, N_COL - 1)
    reverse = 7 - direction
    available = counts[row_at, col_at, reverse]
    slot_pick = raw_slot % available
    grain_id = listed[row_at, col_at, reverse, slot_pick]
    is_ghost = (wanted == 1) & inside
    halo_block = jnp.where(direction < 4, direction, direction + 1)
    sdf_rows = jnp.where(is_ghost, GR_DEV + direction * GHOST + slot_pick, partner)
    pose_rows = jnp.where(is_ghost, halo_block * GR_DEV + grain_id, 4 * GR_DEV + partner)
    return (listed, owner_grain.reshape(-1), sdf_rows.reshape(-1), pose_rows.reshape(-1))


def draw_send_list(key, part):
    return layout(key)[0].astype(jnp.int32)


def draw_pair_first(key, part):
    return layout(key)[1].astype(jnp.int32)


def draw_pair_sdf(key, part):
    return layout(key)[2].astype(jnp.int32)


def draw_pair_pose(key, part):
    return layout(key)[3].astype(jnp.int32)


def draw_pair_live(key, part):
    devices = N_ROW * N_COL
    halving = jax.random.randint(jax.random.fold_in(key, 201), (devices,), 0, 3)
    live_count = jnp.right_shift(jnp.full((devices,), PAIRS_DEV, jnp.int32), halving)
    busiest = jax.random.randint(jax.random.fold_in(key, 202), (1,), 0, devices)
    live_count = jnp.where(jnp.arange(devices, dtype=jnp.int32) == busiest, PAIRS_DEV, live_count)
    live = jnp.arange(PAIRS_DEV, dtype=jnp.int32)[None, :] < live_count[:, None]
    return live.astype(jnp.int32).reshape(-1)


def set_ends(result, own_key, smallest, largest):
    extent = result.shape
    place = [jax.random.randint(jax.random.fold_in(own_key, axis), (), 0, extent[axis]) for axis in range(len(extent))]
    result = result.at[tuple(place)].set(smallest)
    longest = extent.index(max(extent))
    place[longest] = (place[longest] + 1) % extent[longest]
    return result.at[tuple(place)].set(largest)


def steps_of(rng, shape, cuts, low, top_value):
    level = 1.0
    for dim, shards_of in cuts:
        draws = jax.random.uniform(jax.random.fold_in(jax.random.fold_in(rng, 6), dim), (shards_of,), jnp.float32, low / len(cuts), top_value / len(cuts))
        level = level * jnp.repeat(jnp.exp(draws), shape[dim] // shards_of).reshape((-1,) + (1,) * (len(shape) - 1 - dim))
    return level


def bell_draw(key, dims, spread, reach, cuts=(), held_as=jnp.bfloat16):
    values = spread * jax.random.normal(key, dims, jnp.float32)
    if cuts:
        values = values * steps_of(key, dims, cuts, -0.22, 0.18)
    return jnp.clip(values, -reach, reach).astype(held_as)


def setup_inputs(seed: int = 0) -> dict:
    keys = jax.random.split(jax.random.key(seed), 11)
    sdf_grids = bell_draw(keys[0], (GRAINS, GRID * GRID * GRID), 1.0, 6.0, ((0, 128),))
    grain_poses = bell_draw(keys[1], (12, GRAINS), 0.6, 4.0, ((1, 128),), jnp.float32)
    surface_nodes = bell_draw(keys[2], (GRAINS, 3 * NODES), 1.0, 5.0, ((0, 128),), jnp.float32)
    send_list = draw_send_list(jax.random.fold_in(keys[10], 71), 0)
    pair_first = draw_pair_first(jax.random.fold_in(keys[10], 71), 0)
    pair_sdf = draw_pair_sdf(jax.random.fold_in(keys[10], 71), 0)
    pair_pose = draw_pair_pose(jax.random.fold_in(keys[10], 71), 0)
    pair_live = draw_pair_live(jax.random.fold_in(keys[10], 71), 0)
    knot_cells = set_ends(jax.random.randint(keys[8], (PAIRS, 3 * NODES), 1, GRID - 2), jax.random.fold_in(keys[8], 1), 1, (GRID - 2) - 1).astype(jnp.int32)
    offsets = jnp.clip(1.0 * jax.random.uniform(keys[9], (PAIRS, 3 * NODES), jnp.float32) ** steps_of(keys[9], (PAIRS, 3 * NODES), ((0, 128),), -0.2, 0.2), 0.0, 1.0)
    return dict(sdf_grids=sdf_grids, grain_poses=grain_poses, surface_nodes=surface_nodes, send_list=send_list, pair_first=pair_first, pair_sdf=pair_sdf, pair_pose=pair_pose, pair_live=pair_live, knot_cells=knot_cells, offsets=offsets)


DIRECTIONS = ((-1, -1), (-1, 0), (-1, 1), (0, -1), (0, 1), (1, -1), (1, 0), (1, 1))
STIFFNESS = 0.25
pair_block = 32


def spline_tables(knot_cell, fraction):
    complement = 1.0 - fraction
    squared = fraction * fraction
    cubed = squared * fraction
    weights = (complement * complement * complement / 6.0, (3.0 * cubed - 6.0 * squared + 4.0) / 6.0,
               (-3.0 * cubed + 3.0 * squared + 3.0 * fraction + 1.0) / 6.0, cubed / 6.0)
    slopes = (-0.5 * complement * complement, 0.5 * (3.0 * squared - 4.0 * fraction),
              0.5 * (-3.0 * squared + 2.0 * fraction + 1.0), 0.5 * squared)
    cell_ids = jnp.arange(GRID, dtype=jnp.int32)[:, None]
    shape = knot_cell.shape[:2] + (GRID,) + knot_cell.shape[2:]
    basis_rows = jnp.zeros(shape, jnp.float32)
    slope_rows = jnp.zeros(shape, jnp.float32)
    for position in range(4):
        matches = cell_ids == (knot_cell + (position - 1))[:, :, None, :]
        basis_rows = basis_rows + jnp.where(matches, weights[position][:, :, None, :], jnp.float32(0.0))
        slope_rows = slope_rows + jnp.where(matches, slopes[position][:, :, None, :], jnp.float32(0.0))
    return basis_rows, slope_rows


def pair_terms(grid_rows, knot_cell, fraction, pose_first, pose_second, node_body):
    highest = lax.Precision.HIGHEST
    batch_size = grid_rows.shape[0]
    node_count = knot_cell.shape[2]
    basis_rows, slope_rows = spline_tables(knot_cell, fraction)
    x_basis = basis_rows[:, 0].astype(jnp.bfloat16).astype(jnp.float32)
    x_slope = slope_rows[:, 0].astype(jnp.bfloat16).astype(jnp.float32)
    grid_cube = grid_rows.reshape(batch_size, GRID, GRID * GRID).astype(jnp.float32)
    partial_plain = jnp.einsum("pam,pan->pmn", grid_cube, x_basis, precision=highest).reshape(batch_size, GRID, GRID, node_count)
    partial_slope = jnp.einsum("pam,pan->pmn", grid_cube, x_slope, precision=highest).reshape(batch_size, GRID, GRID, node_count)
    basis_y = basis_rows[:, 1]
    slope_y = slope_rows[:, 1]
    section_plain = jnp.einsum("pbcn,pbn->pcn", partial_plain, basis_y, precision=highest)
    section_xslope = jnp.einsum("pbcn,pbn->pcn", partial_slope, basis_y, precision=highest)
    section_yslope = jnp.einsum("pbcn,pbn->pcn", partial_plain, slope_y, precision=highest)
    basis_z = basis_rows[:, 2]
    slope_z = slope_rows[:, 2]
    distance = jnp.einsum("pcn,pcn->pn", section_plain, basis_z, precision=highest)
    gradient = jnp.stack([jnp.einsum("pcn,pcn->pn", section_xslope, basis_z, precision=highest),
                          jnp.einsum("pcn,pcn->pn", section_yslope, basis_z, precision=highest),
                          jnp.einsum("pcn,pcn->pn", section_plain, slope_z, precision=highest)], axis=1)
    penetration = STIFFNESS * jax.nn.relu(-distance)
    rotation_second = pose_second[:, 3:].reshape(batch_size, 3, 3)
    rotation_first = pose_first[:, 3:].reshape(batch_size, 3, 3)
    normal = jnp.einsum("prc,pcn->prn", rotation_second, gradient, precision=highest)
    node_force = penetration[:, None, :] * normal
    lever_arm = jnp.einsum("prc,pcn->prn", rotation_first, node_body, precision=highest)
    net_force = jnp.sum(node_force, axis=2)
    moment = jnp.sum(jnp.cross(lever_arm, node_force, axis=1), axis=2)
    separation = pose_first[:, :3] - pose_second[:, :3]
    moment_other = -(jnp.cross(separation, net_force, axis=1) + moment)
    return jnp.concatenate([net_force, moment], axis=1), jnp.concatenate([-net_force, moment_other], axis=1)


def pair_loads(grid_table, pose_table, grain_poses, surface_nodes, pair_first, pair_sdf, pair_pose, pair_live, knot_cells, offsets):
    pair_count = pair_first.shape[0]
    node_count = knot_cells.shape[1] // 3
    block_size = min(pair_block, pair_count)
    grid_rows = jnp.take(grid_table, pair_sdf, axis=0)
    pose_first = jnp.take(grain_poses, pair_first, axis=1).T
    pose_second = jnp.take(pose_table, pair_pose, axis=1).T
    node_body = jnp.take(surface_nodes, pair_first, axis=0).reshape(pair_count, 3, node_count)
    knot_cell = knot_cells.reshape(pair_count, 3, node_count)
    fraction = offsets.reshape(pair_count, 3, node_count)
    pieces = (grid_rows, knot_cell, fraction, pose_first, pose_second, node_body)
    blocked = tuple(item.reshape((pair_count // block_size, block_size) + item.shape[1:]) for item in pieces)
    on_first, on_second = lax.map(lambda group: pair_terms(*group), blocked)
    alive_mask = pair_live.astype(jnp.float32)[:, None]
    on_first = on_first.reshape(pair_count, 6) * alive_mask
    on_second = on_second.reshape(pair_count, 6) * alive_mask
    return jax.ops.segment_sum(jnp.concatenate([on_first, on_second], axis=0),
                               jnp.concatenate([pair_first, pair_sdf], axis=0).astype(jnp.int32),
                               num_segments=grid_table.shape[0])


def shift_grid(field, row_step, col_step):
    padded = jnp.pad(field, ((1, 1), (1, 1)) + ((0, 0),) * (field.ndim - 2))
    return padded[1 + row_step:1 + row_step + N_ROW, 1 + col_step:1 + col_step + N_COL]


def reference(sdf_grids, grain_poses, surface_nodes, send_list, pair_first, pair_sdf, pair_pose, pair_live, knot_cells, offsets):
    devices = N_ROW * N_COL
    cells = sdf_grids.shape[1]
    grids_dev = sdf_grids.reshape(devices, GR_DEV, cells)
    listed = send_list.reshape(devices, 8 * GHOST)
    outgoing = jax.vmap(lambda grid_set, chosen: jnp.take(grid_set, chosen, axis=0))(grids_dev, listed)
    outgoing = outgoing.reshape(N_ROW, N_COL, 8, GHOST, cells)
    received = jnp.stack([shift_grid(outgoing[:, :, 7 - direction], DIRECTIONS[direction][0], DIRECTIONS[direction][1])
                          for direction in range(8)], axis=2)
    grid_table = jnp.concatenate([grids_dev.reshape(N_ROW, N_COL, GR_DEV, cells),
                                  received.reshape(N_ROW, N_COL, 8 * GHOST, cells)], axis=2)
    grid_table = grid_table.reshape(devices, GR_DEV + 8 * GHOST, cells)
    pose_dev = grain_poses.reshape(12, N_ROW, N_COL, GR_DEV).transpose(1, 2, 0, 3)
    pose_table = jnp.stack([shift_grid(pose_dev, row_step, col_step) for row_step in (-1, 0, 1) for col_step in (-1, 0, 1)], axis=3)
    pose_table = pose_table.reshape(devices, 12, 9 * GR_DEV)
    slot_sums = lax.map(lambda pieces: pair_loads(*pieces),
                        (grid_table, pose_table, pose_dev.reshape(devices, 12, GR_DEV),
                         surface_nodes.reshape(devices, GR_DEV, -1), pair_first.reshape(devices, -1),
                         pair_sdf.reshape(devices, -1), pair_pose.reshape(devices, -1), pair_live.reshape(devices, -1),
                         knot_cells.reshape(devices, PAIRS_DEV, -1), offsets.reshape(devices, PAIRS_DEV, -1)))
    owned_sum = slot_sums[:, :GR_DEV]
    reaction = slot_sums[:, GR_DEV:].reshape(N_ROW, N_COL, 8, GHOST, 6)
    returned = jnp.stack([shift_grid(reaction[:, :, 7 - direction], DIRECTIONS[direction][0], DIRECTIONS[direction][1])
                          for direction in range(8)], axis=2).reshape(devices, 8 * GHOST, 6)
    owned_sum = owned_sum + jax.vmap(lambda loads, chosen: jax.ops.segment_sum(loads, chosen, num_segments=GR_DEV))(returned, listed)
    return owned_sum.transpose(2, 0, 1).reshape(6, devices * GR_DEV)
```

```python
import functools

import jax
import jax.numpy as jnp
from jax import lax
from jax.experimental import pallas as pl
from jax.experimental.pallas import tpu as pltpu
from jax.sharding import PartitionSpec as P

GRID = 16
STIFFNESS = 0.25
OPS = ("C", "D", "AC", "AD", "BC", "BD", "A", "B")
F32 = jnp.float32
BF16 = jnp.bfloat16
NN = (((1,), (0,)), ((), ()))
NT = (((1,), (1,)), ((), ()))


def steps_of(op):
    row = 1 if "A" in op else (-1 if "B" in op else 0)
    col = 1 if "C" in op else (-1 if "D" in op else 0)
    return row, col


def direction_of(row_step, col_step):
    cell = (row_step + 1) * 3 + col_step + 1
    return cell - (cell > 4).astype(jnp.int32)


def parity_signs():
    return 1 - 2 * (lax.axis_index("row") & 1), 1 - 2 * (lax.axis_index("col") & 1)


def split3(value):
    high = value.astype(BF16)
    rest = value - high.astype(F32)
    middle = rest.astype(BF16)
    low = (rest - middle.astype(F32)).astype(BF16)
    return high, middle, low


def dot(left, right, dims=NN):
    return lax.dot_general(left, right, dims, preferred_element_type=F32)


def listed_column(listed, signs, op):
    row_step, col_step = steps_of(op)
    direction = direction_of(row_step * signs[0], col_step * signs[1])
    row = listed[pl.ds(direction, 1), :].astype(F32)
    size = row.shape[1]
    eye = lax.broadcasted_iota(jnp.int32, (size, size), 0) == lax.broadcasted_iota(jnp.int32, (size, size), 1)
    return jnp.sum(jnp.where(eye, row, 0.0), axis=1, keepdims=True)


def one_hot_rows(column, width):
    lanes = lax.broadcasted_iota(jnp.int32, (column.shape[0], width), 1).astype(F32)
    return jnp.where(lanes == column, 1.0, 0.0).astype(BF16)


def pose_pieces(poses, pieces, padded):
    padded[...] = jnp.zeros_like(padded)
    padded[0:12, :] = poses[...]
    for index, piece in enumerate(split3(padded[...])):
        pieces[16 * index:16 * index + 16, :] = piece


def pack_kernel(listed, poses, grids, *refs):
    outs = refs[:8]
    table, hot, padded, pieces, sems = refs[8:]
    chunks = sems.shape[0]
    width = grids.shape[1] // chunks
    copies = []
    for index in range(chunks):
        part = pl.ds(index * width, width)
        copy = pltpu.make_async_copy(grids.at[:, part], table.at[:, part], sems.at[index])
        copy.start()
        copies.append(copy)
    signs = parity_signs()
    grains = grids.shape[0]
    for index, op in enumerate(OPS):
        hot[32 * index:32 * index + 32, :] = one_hot_rows(listed_column(listed, signs, op), grains)
    pieces[...] = jnp.zeros_like(pieces)
    pose_pieces(poses, pieces, padded)
    chosen = dot(hot[...], pieces[...], NT).astype(BF16)
    for index in range(8):
        outs[index][:, chunks * width:] = chosen[32 * index:32 * index + 32]
    for step in range(chunks):
        copies[step].wait()
        part = slice(step * width, step * width + width)
        rows = dot(hot[...], table[:, part]).astype(BF16)
        for index in range(8):
            outs[index][:, part] = rows[32 * index:32 * index + 32]


def pack(listed, poses, grids):
    grains, cells = grids.shape
    vmem = pl.BlockSpec(memory_space=pltpu.VMEM)
    return pl.pallas_call(
        pack_kernel,
        out_shape=[jax.ShapeDtypeStruct((32, cells + 128), BF16)] * 8,
        in_specs=[vmem, vmem, pl.BlockSpec(memory_space=pl.ANY)],
        out_specs=[vmem] * 8,
        scratch_shapes=[
            pltpu.VMEM((grains, cells), BF16),
            pltpu.VMEM((256, grains), BF16),
            pltpu.VMEM((16, grains), F32),
            pltpu.VMEM((128, grains), BF16),
            pltpu.SemaphoreType.DMA((4,)),
        ],
        name="pack",
    )(listed, poses, grids)


def spline(position):
    cells = lax.broadcasted_iota(jnp.int32, (GRID, position.shape[1]), 0).astype(F32)
    offset = position - cells
    distance = jnp.abs(offset)
    outer = 2.0 - distance
    inner = jnp.maximum(outer - distance, 0.0)
    outer = jnp.maximum(outer, 0.0)
    outer_sq = outer * outer
    inner_sq = inner * inner
    basis6 = outer_sq * outer - 0.5 * (inner_sq * inner)
    bend = inner_sq - outer_sq
    return basis6, jnp.where(offset < 0.0, -bend, bend)


def spread_rows(grid_rows, cell, values):
    for half in range(2):
        grid_rows[half, pl.ds(cell, values.shape[0], stride=GRID), :] = values[:, 128 * half:128 * half + 128]


def pair_partials(slot, pair, grid_rows, positions, product, partial):
    nodes = positions.shape[1] // 3
    cube_rows = pl.ds(pl.multiple_of(pair * GRID, GRID), GRID)
    cube = jnp.concatenate([grid_rows[half, cube_rows, :].astype(BF16) for half in range(2)], axis=1)
    spots = [positions[pl.ds(pair, 1), axis * nodes:axis * nodes + nodes] for axis in range(3)]
    basis_y, slope_y = spline(spots[1])
    basis_z, slope_z = spline(spots[2])
    for cell in range(GRID):
        plain = jnp.broadcast_to(basis_y[cell:cell + 1], basis_z.shape)
        tilt = jnp.broadcast_to(slope_y[cell:cell + 1], basis_z.shape)
        rows = slice(cell * GRID, cell * GRID + GRID)
        product[rows, 0:nodes] = (plain * basis_z).astype(BF16)
        product[rows, nodes:2 * nodes] = (tilt * basis_z).astype(BF16)
        product[rows, 2 * nodes:3 * nodes] = (plain * slope_z).astype(BF16)
    basis_x, slope_x = spline(spots[0])
    basis_x = (basis_x * (1.0 / 6.0)).astype(BF16).astype(F32)
    slope_x = (slope_x * 0.5).astype(BF16).astype(F32)
    sums = dot(cube, product[...])
    plain = sums[:, 0:nodes]
    for index, (weight, term) in enumerate(
        ((basis_x, plain), (slope_x, plain), (basis_x, sums[:, nodes:2 * nodes]), (basis_x, sums[:, 2 * nodes:]))
    ):
        both = weight * term
        both = both[0:8] + both[8:16]
        for half in range(2):
            partial[2 * index + half, slot * 8:slot * 8 + 8, :] = both[:, 128 * half:128 * half + 128]


def group_sums(partial, bodies):
    nodes = 2 * partial.shape[2]
    totals = []
    for index in range(4):
        halves = []
        for half in range(2):
            parts = [partial[2 * index + half, pl.ds(part, 8, stride=8), :] for part in range(8)]
            while len(parts) > 1:
                parts = [left + right for left, right in zip(parts[::2], parts[1::2])]
            halves.append(parts[0])
        totals.append(jnp.concatenate(halves, axis=1))
    push = jnp.maximum(-totals[0], 0.0)
    force = [push * totals[1], push * totals[2], push * totals[3]]
    lanes = lax.broadcasted_iota(jnp.int32, (8, 128), 1)
    result = jnp.zeros((8, 128), F32)
    for m in range(3):
        result = jnp.where(lanes == m, jnp.sum(force[m], axis=1, keepdims=True), result)
        for l in range(3):
            product = bodies[:, l * nodes:l * nodes + nodes] * force[m]
            result = jnp.where(lanes == 3 + 3 * l + m, jnp.sum(product, axis=1, keepdims=True), result)
    return result


def pair_loop(count, order, grid_rows, positions, bodies_of, results, product, partial, bodies):
    def group(index, carry):
        pairs = [order[index * 8 + slot] for slot in range(8)]
        for slot in range(8):
            bodies[slot:slot + 1, :] = bodies_of(pairs[slot])
            pair_partials(slot, pairs[slot], grid_rows, positions, product.at[slot % 2], partial)
        sums = group_sums(partial, bodies)
        for slot in range(8):
            results[pl.ds(pairs[slot], 1), :] = sums[slot:slot + 1]
        return carry

    lax.fori_loop(0, (count + 7) // 8, group, 0)


def own_kernel(first_s, sdf_s, live_s, first, sdf, listed, poses, grids, body_table, knots, offsets,
               results, positions, bodies_out, pose_pairs, targets, order_out,
               grid_rows, own_order, product, partial, bodies, padded, pieces):
    pairs, width = positions.shape
    grains = body_table.shape[0]
    signs = parity_signs()

    def sort_pair(pair, counts):
        own, ghost = counts
        live = live_s[pair]
        near = jnp.where(sdf_s[pair] < grains, 1, 0)
        own_order[own] = pair
        order_out[ghost] = pair
        return own + live * near, ghost + live * (1 - near)

    own, ghost = lax.fori_loop(0, pairs, sort_pair, (0, 0))
    own_last = own_order[jnp.maximum(own - 1, 0)]
    ghost_last = order_out[jnp.maximum(ghost - 1, 0)]
    for extra in range(8):
        own_order[own + extra] = own_last
        order_out[ghost + extra] = ghost_last
    order_out[143] = ghost

    results[...] = jnp.zeros_like(results)
    positions[...] = knots[...].astype(F32) + offsets[...]

    def copy_body(pair, carry):
        bodies_out[pl.ds(pair, 1), :] = body_table[pl.ds(first_s[pair], 1), :]
        return carry

    lax.fori_loop(0, pairs, copy_body, 0, unroll=8)

    rows = lax.broadcasted_iota(jnp.int32, (grains, pairs), 0)
    first_hot = jnp.where(rows == first[...], 1.0, 0.0).astype(BF16)
    sdf_hot32 = jnp.where(rows == sdf[...], 1.0, 0.0)
    pose_pieces(poses, pieces, padded)
    pose_pairs[0:48, :] = dot(pieces[...], first_hot)
    pose_pairs[48:96, :] = dot(pieces[...], sdf_hot32.astype(BF16))
    hot = sdf_hot32.T.astype(BF16)
    for cell in range(GRID):
        part = slice(cell * GRID * GRID, cell * GRID * GRID + GRID * GRID)
        spread_rows(grid_rows, cell, dot(hot, grids[:, part]))

    targets[...] = jnp.zeros_like(targets)
    for base, op in ((0, "A"), (128, "B"), (256, "C"), (288, "AC"), (320, "BC"), (384, "D"), (416, "BD"), (448, "AD")):
        targets[base:base + 32, :] = one_hot_rows(listed_column(listed, signs, op), grains)

    pair_loop(own, own_order, grid_rows, positions, lambda pair: bodies_out[pl.ds(pair, 1), :],
              results, product, partial, bodies)


def own_pairs(first, sdf, live, listed, poses, grids, body_table, knots, offsets):
    pairs, width = knots.shape
    grains, cells = grids.shape
    vmem = pl.BlockSpec(memory_space=pltpu.VMEM)
    smem = pl.BlockSpec(memory_space=pltpu.SMEM)
    return pl.pallas_call(
        own_kernel,
        out_shape=[
            jax.ShapeDtypeStruct((pairs, 128), F32),
            jax.ShapeDtypeStruct((pairs, width), F32),
            jax.ShapeDtypeStruct((pairs, width), F32),
            jax.ShapeDtypeStruct((96, pairs), F32),
            jax.ShapeDtypeStruct((512, grains), BF16),
            jax.ShapeDtypeStruct((144,), jnp.int32),
        ],
        in_specs=[smem] * 3 + [vmem] * 8,
        out_specs=[vmem] * 5 + [smem],
        scratch_shapes=[
            pltpu.VMEM((2, pairs * GRID, 128), F32),
            pltpu.SMEM((144,), jnp.int32),
            pltpu.VMEM((2, GRID * GRID, width), BF16),
            pltpu.VMEM((8, 64, 128), F32),
            pltpu.VMEM((8, width), F32),
            pltpu.VMEM((16, grains), F32),
            pltpu.VMEM((48, grains), BF16),
        ],
        cost_estimate=pl.CostEstimate(flops=6 * 10**9, bytes_accessed=16 * 10**6, transcendentals=0),
        name="own_pairs",
    )(first, sdf, live, first.reshape(1, pairs), sdf.reshape(1, pairs), listed, poses, grids, body_table, knots, offsets)


def joined(value, base):
    return value[base:base + 12] + value[base + 16:base + 28] + value[base + 32:base + 44]


def ghost_kernel(order, first, sdf, own_results, positions, bodies_in, pose_pairs, *refs):
    payloads = refs[:8]
    own_sum, load_a, load_b, load_c, load_d = refs[8:13]
    ghosts, results, grid_rows, product, partial, bodies = refs[13:]
    pairs = positions.shape[0]
    grains = own_sum.shape[1]
    cells = GRID * GRID * GRID
    signs = parity_signs()
    for index in range(8):
        ghosts[32 * index:32 * index + 32, :] = payloads[index][...]

    row = sdf[...]
    ghost = row - grains
    direction = jnp.right_shift(ghost, 5)
    slot = jnp.bitwise_and(ghost, 31)
    cell = direction + jnp.where(direction >= 4, 1, 0)
    third = jnp.where(cell >= 6, 2, jnp.where(cell >= 3, 1, 0))
    row_step = (third - 1) * signs[0]
    col_step = (cell - 3 * third - 1) * signs[1]
    buffer_row = jnp.zeros_like(row)
    place = jnp.zeros_like(row)
    bases = {"A": 0, "AC": 32, "AD": 64, "B": 128, "BD": 160, "BC": 192, "C": 256, "D": 384}
    for index, op in enumerate(OPS):
        row_want, col_want = steps_of(op)
        match = (row_step == row_want) & (col_step == col_want)
        buffer_row = jnp.where(match, 32 * index, buffer_row)
        place = jnp.where(match, bases[op], place)
    buffer_row = jnp.where(ghost >= 0, buffer_row + slot, -1)
    place = jnp.where(ghost >= 0, place + slot, -1)

    slot_rows = lax.broadcasted_iota(jnp.int32, (256, pairs), 0)
    slot_hot = jnp.where(slot_rows == buffer_row, 1.0, 0.0)
    hot = slot_hot.T.astype(BF16)
    for index in range(GRID):
        part = slice(index * GRID * GRID, index * GRID * GRID + GRID * GRID)
        spread_rows(grid_rows, index, dot(hot, ghosts[:, part]))
    ghost_pose = dot(ghosts[:, cells:].astype(F32).T.astype(BF16), slot_hot.astype(BF16))

    results[...] = own_results[...]
    pair_loop(order[143], order, grid_rows, positions, lambda pair: bodies_in[pl.ds(pair, 1), :],
              results, product, partial, bodies)

    sums = results[...].T
    pose_first = joined(pose_pairs[...], 0)
    pose_second = joined(pose_pairs[...], 48) + joined(ghost_pose, 0)
    take = lambda value, index: value[index:index + 1]
    total = [take(sums, m) * SCALES[m] for m in range(3)]
    moment = [[take(sums, 3 + 3 * l + m) * SCALES[m] for m in range(3)] for l in range(3)]
    turn_1 = [[take(pose_first, 3 + 3 * i + j) for j in range(3)] for i in range(3)]
    turn_2 = [[take(pose_second, 3 + 3 * i + j) for j in range(3)] for i in range(3)]
    apart = [take(pose_first, i) - take(pose_second, i) for i in range(3)]
    force = [turn_2[i][0] * total[0] + turn_2[i][1] * total[1] + turn_2[i][2] * total[2] for i in range(3)]
    half = [[turn_1[j][0] * moment[0][m] + turn_1[j][1] * moment[1][m] + turn_1[j][2] * moment[2][m]
             for m in range(3)] for j in range(3)]
    outer = [[half[j][0] * turn_2[k][0] + half[j][1] * turn_2[k][1] + half[j][2] * turn_2[k][2]
              for k in range(3)] for j in range(3)]
    first_moment = [outer[1][2] - outer[2][1], outer[2][0] - outer[0][2], outer[0][1] - outer[1][0]]
    crossed = [apart[1] * force[2] - apart[2] * force[1], apart[2] * force[0] - apart[0] * force[2],
               apart[0] * force[1] - apart[1] * force[0]]
    second_moment = [-(crossed[i] + first_moment[i]) for i in range(3)]
    zero = jnp.zeros_like(force[0])
    loads_1 = jnp.concatenate(force + first_moment + [zero, zero], axis=0)
    loads_2 = jnp.concatenate([-value for value in force] + second_moment + [zero, zero], axis=0)
    loads_1 = jnp.concatenate(split3_rows(loads_1), axis=0).astype(BF16)
    loads_2 = jnp.concatenate(split3_rows(loads_2), axis=0).astype(BF16)
    rows = lax.broadcasted_iota(jnp.int32, (grains, pairs), 0)
    first_hot = jnp.where(rows == first[...], 1.0, 0.0).astype(BF16)
    own_hot = jnp.where(rows == row, 1.0, 0.0).astype(BF16)
    place_hot = jnp.where(rows == place, 1.0, 0.0).astype(BF16)
    near = dot(loads_1, first_hot, NT) + dot(loads_2, own_hot, NT)
    own_sum[...] = near[0:8] + near[8:16] + near[16:24]
    far = dot(loads_2, place_hot, NT)
    far = far[0:8] + far[8:16] + far[16:24]
    for index, out in enumerate((load_a, load_b, load_c, load_d)):
        out[...] = far[:, 128 * index:128 * index + 128]


SCALES = (STIFFNESS / 1296.0, STIFFNESS / 432.0, STIFFNESS / 432.0)


def split3_rows(value):
    return [piece.astype(F32) for piece in split3(value)]


def ghost_pairs(order, first, sdf, own_results, positions, bodies, pose_pairs, payloads, grains):
    pairs, width = positions.shape
    vmem = pl.BlockSpec(memory_space=pltpu.VMEM)
    smem = pl.BlockSpec(memory_space=pltpu.SMEM)
    load = jax.ShapeDtypeStruct((8, 128), F32)
    return pl.pallas_call(
        ghost_kernel,
        out_shape=[jax.ShapeDtypeStruct((8, grains), F32)] + [load] * 4,
        in_specs=[smem] + [vmem] * 14,
        out_specs=[vmem] * 5,
        scratch_shapes=[
            pltpu.VMEM((256, payloads[0].shape[1]), BF16),
            pltpu.VMEM((pairs, 128), F32),
            pltpu.VMEM((2, pairs * GRID, 128), F32),
            pltpu.VMEM((2, GRID * GRID, width), BF16),
            pltpu.VMEM((8, 64, 128), F32),
            pltpu.VMEM((8, width), F32),
        ],
        name="ghost_pairs",
    )(order, first.reshape(1, pairs), sdf.reshape(1, pairs), own_results, positions, bodies, pose_pairs, *payloads)


def return_kernel(own_sum, load_a, load_b, load_c, load_d, targets, out):
    loads = jnp.concatenate([load_a[...], load_b[...], load_c[...], load_d[...]], axis=1)
    pieces = jnp.concatenate(split3_rows(loads), axis=0).astype(BF16)
    added = dot(pieces, targets[...])
    total = own_sum[...] + (added[0:8] + added[8:16] + added[16:24])
    out[...] = total[0:6]


def return_loads(own_sum, loads, targets):
    vmem = pl.BlockSpec(memory_space=pltpu.VMEM)
    return pl.pallas_call(
        return_kernel,
        out_shape=jax.ShapeDtypeStruct((6, own_sum.shape[1]), F32),
        in_specs=[vmem] * 6,
        out_specs=vmem,
        name="return_loads",
    )(own_sum, *loads, targets)


def swapped(block, op, rows, cols):
    route = []
    row_step, col_step = steps_of(op)
    for r in range(rows):
        for c in range(cols):
            to_r = r + row_step * (1 - 2 * (r % 2))
            to_c = c + col_step * (1 - 2 * (c % 2))
            if 0 <= to_r < rows and 0 <= to_c < cols:
                route.append((r * cols + c, to_r * cols + to_c))
    return lax.ppermute(block, ("row", "col"), route)


def local(rows, cols, sdf_grids, grain_poses, surface_nodes, send_list, pair_first, pair_sdf, pair_pose, pair_live,
          knot_cells, offsets):
    grains = sdf_grids.shape[0]
    listed = send_list.reshape(8, send_list.shape[3])
    swap = lambda block, op: swapped(block, op, rows, cols)
    packed = pack(listed, grain_poses, sdf_grids)
    payloads = [swap(block, op) for block, op in zip(packed, OPS)]
    results, positions, bodies, pose_pairs, targets, order = own_pairs(
        pair_first, pair_sdf, pair_live, listed, grain_poses, sdf_grids, surface_nodes, knot_cells, offsets)
    own_sum, load_a, load_b, load_c, load_d = ghost_pairs(
        order, pair_first, pair_sdf, results, positions, bodies, pose_pairs, payloads, grains)
    back_a, back_b = swap(load_a, "A"), swap(load_b, "B")
    lanes = lax.broadcasted_iota(jnp.int32, load_a.shape, 1)
    send_c = jnp.where(lanes < 32, load_c, jnp.where(lanes < 64, back_a, back_b))
    send_d = jnp.where(lanes < 32, load_d, jnp.where(lanes < 64, back_b, back_a))
    back_c, back_d = swap(send_c, "C"), swap(send_d, "D")
    return return_loads(own_sum, (back_a, back_b, back_c, back_d), targets)


def solution(mesh):
    in_specs = (
        P(("row", "col"), None),
        P(None, ("row", "col")),
        P(("row", "col"), None),
        P("row", "col", None, None),
        P(("row", "col")),
        P(("row", "col")),
        P(("row", "col")),
        P(("row", "col")),
        P(("row", "col"), None),
        P(("row", "col"), None),
    )
    out_specs = P(None, ("row", "col"))
    body = functools.partial(local, mesh.shape["row"], mesh.shape["col"])
    return jax.shard_map(body, mesh=mesh, in_specs=in_specs, out_specs=out_specs, check_vma=False)
```

```python
import functools

import jax
import jax.numpy as jnp
from jax import lax
from jax.experimental import pallas as pl
from jax.experimental.pallas import tpu as pltpu
from jax.sharding import PartitionSpec as P

GRID = 16
STIFFNESS = 0.25
OPS = ("C", "D", "AC", "AD", "BC", "BD", "A", "B")
F32 = jnp.float32
BF16 = jnp.bfloat16
NN = (((1,), (0,)), ((), ()))
NT = (((1,), (1,)), ((), ()))


def steps_of(op):
    row = 1 if "A" in op else (-1 if "B" in op else 0)
    col = 1 if "C" in op else (-1 if "D" in op else 0)
    return row, col


def direction_of(row_step, col_step):
    cell = (row_step + 1) * 3 + col_step + 1
    return cell - (cell > 4).astype(jnp.int32)


def parity_signs():
    return 1 - 2 * (lax.axis_index("row") & 1), 1 - 2 * (lax.axis_index("col") & 1)


def split3(value):
    high = value.astype(BF16)
    rest = value - high.astype(F32)
    middle = rest.astype(BF16)
    low = (rest - middle.astype(F32)).astype(BF16)
    return high, middle, low


def dot(left, right, dims=NN):
    return lax.dot_general(left, right, dims, preferred_element_type=F32)


def listed_column(listed, signs, op):
    row_step, col_step = steps_of(op)
    direction = direction_of(row_step * signs[0], col_step * signs[1])
    row = listed[pl.ds(direction, 1), :].astype(F32)
    size = row.shape[1]
    eye = lax.broadcasted_iota(jnp.int32, (size, size), 0) == lax.broadcasted_iota(jnp.int32, (size, size), 1)
    return jnp.sum(jnp.where(eye, row, 0.0), axis=1, keepdims=True)


def one_hot_rows(column, width):
    lanes = lax.broadcasted_iota(jnp.int32, (column.shape[0], width), 1).astype(F32)
    return jnp.where(lanes == column, 1.0, 0.0).astype(BF16)


def pose_pieces(poses, pieces, padded):
    padded[...] = jnp.zeros_like(padded)
    padded[0:12, :] = poses[...]
    for index, piece in enumerate(split3(padded[...])):
        pieces[16 * index:16 * index + 16, :] = piece


def pack_kernel(listed, poses, grids, *refs):
    outs = refs[:8]
    table, hot, padded, pieces, sems = refs[8:]
    chunks = sems.shape[0]
    width = grids.shape[1] // chunks
    copies = []
    for index in range(chunks):
        part = pl.ds(index * width, width)
        copy = pltpu.make_async_copy(grids.at[:, part], table.at[:, part], sems.at[index])
        copy.start()
        copies.append(copy)
    signs = parity_signs()
    grains = grids.shape[0]
    for index, op in enumerate(OPS):
        hot[32 * index:32 * index + 32, :] = one_hot_rows(listed_column(listed, signs, op), grains)
    pieces[...] = jnp.zeros_like(pieces)
    pose_pieces(poses, pieces, padded)
    chosen = dot(hot[...], pieces[...], NT).astype(BF16)
    for index in range(8):
        outs[index][:, chunks * width:] = chosen[32 * index:32 * index + 32]
    for step in range(chunks):
        copies[step].wait()
        part = slice(step * width, step * width + width)
        rows = dot(hot[...], table[:, part]).astype(BF16)
        for index in range(8):
            outs[index][:, part] = rows[32 * index:32 * index + 32]


def pack(listed, poses, grids):
    grains, cells = grids.shape
    vmem = pl.BlockSpec(memory_space=pltpu.VMEM)
    return pl.pallas_call(
        pack_kernel,
        out_shape=[jax.ShapeDtypeStruct((32, cells + 128), BF16)] * 8,
        in_specs=[vmem, vmem, pl.BlockSpec(memory_space=pl.ANY)],
        out_specs=[vmem] * 8,
        scratch_shapes=[
            pltpu.VMEM((grains, cells), BF16),
            pltpu.VMEM((256, grains), BF16),
            pltpu.VMEM((16, grains), F32),
            pltpu.VMEM((128, grains), BF16),
            pltpu.SemaphoreType.DMA((4,)),
        ],
        name="pack",
    )(listed, poses, grids)


def weight_rows(spots, weights):
    nodes = spots.shape[1] // 3
    knot = jnp.floor(spots[...])
    u = spots[...] - knot
    v = 1.0 - u
    u2 = u * u
    u3 = u2 * u
    v2 = v * v
    rows = [
        v2 * v * (1.0 / 6.0),
        0.5 * u3 - u2 + 2.0 / 3.0,
        0.5 * (u2 + u - u3) + 1.0 / 6.0,
        u3 * (1.0 / 6.0),
        -0.5 * v2,
        1.5 * u2 - 2.0 * u,
        -1.5 * u2 + u + 0.5,
        0.5 * u2,
    ]
    weights[0:8, :] = knot - 1.0
    for index, row in enumerate(rows):
        part = slice(8 * index + 8, 8 * index + 16)
        weights[part, 0:nodes] = row[:, 0:nodes].astype(BF16).astype(F32)
        weights[part, nodes:] = row[:, nodes:]


def spline(weights, slot, axis):
    nodes = weights.shape[1] // 3
    row = lambda index: weights[8 * index + slot:8 * index + slot + 1, axis * nodes:axis * nodes + nodes]
    cells = lax.broadcasted_iota(jnp.int32, (GRID, nodes), 0).astype(F32)
    place = cells - row(0)
    at = [place == float(index) for index in range(4)]
    result = []
    for first in (1, 5):
        value = jnp.where(at[3], row(first + 3), 0.0)
        for index in (2, 1, 0):
            value = jnp.where(at[index], row(first + index), value)
        result.append(value)
    return result


def spread_rows(grid_rows, cell, values):
    for half in range(2):
        grid_rows[half, pl.ds(cell, values.shape[0], stride=GRID), :] = values[:, 128 * half:128 * half + 128]


def pair_partials(slot, pair, grid_rows, weights, spread, product, partial):
    nodes = weights.shape[1] // 3
    cube_rows = pl.ds(pl.multiple_of(pair * GRID, GRID), GRID)
    cube = jnp.concatenate([grid_rows[half, cube_rows, :].astype(BF16) for half in range(2)], axis=1)
    spread[0:GRID, :], spread[GRID:2 * GRID, :] = spline(weights, slot, 1)
    basis_z, slope_z = spline(weights, slot, 2)
    for cell in range(GRID):
        plain = spread[cell:cell + 1, :]
        tilt = spread[GRID + cell:GRID + cell + 1, :]
        rows = slice(cell * GRID, cell * GRID + GRID)
        product[rows, 0:nodes] = (plain * basis_z).astype(BF16)
        product[rows, nodes:2 * nodes] = (tilt * basis_z).astype(BF16)
        product[rows, 2 * nodes:3 * nodes] = (plain * slope_z).astype(BF16)
    basis_x, slope_x = spline(weights, slot, 0)
    sums = dot(cube, product[...])
    plain = sums[:, 0:nodes]
    for index, (weight, term) in enumerate(
        ((basis_x, plain), (slope_x, plain), (basis_x, sums[:, nodes:2 * nodes]), (basis_x, sums[:, 2 * nodes:]))
    ):
        both = weight * term
        both = both[0:8] + both[8:16]
        for half in range(2):
            partial[2 * index + half, slot * 8:slot * 8 + 8, :] = both[:, 128 * half:128 * half + 128]


def group_sums(partial, bodies):
    nodes = 2 * partial.shape[2]
    totals = []
    for index in range(4):
        halves = []
        for half in range(2):
            parts = [partial[2 * index + half, pl.ds(part, 8, stride=8), :] for part in range(8)]
            while len(parts) > 1:
                parts = [left + right for left, right in zip(parts[::2], parts[1::2])]
            halves.append(parts[0])
        totals.append(jnp.concatenate(halves, axis=1))
    push = jnp.maximum(-totals[0], 0.0)
    force = [push * totals[1], push * totals[2], push * totals[3]]
    lanes = lax.broadcasted_iota(jnp.int32, (8, 128), 1)
    result = jnp.zeros((8, 128), F32)
    for m in range(3):
        result = jnp.where(lanes == m, jnp.sum(force[m], axis=1, keepdims=True), result)
        for l in range(3):
            product = bodies[:, l * nodes:l * nodes + nodes] * force[m]
            result = jnp.where(lanes == 3 + 3 * l + m, jnp.sum(product, axis=1, keepdims=True), result)
    return result


def pair_loop(count, order, grid_rows, positions, bodies_in, results, scratch):
    spots, weights, spread, product, partial, bodies = scratch

    def group(index, carry):
        pairs = [order[index * 8 + slot] for slot in range(8)]
        for slot in range(8):
            spots[slot:slot + 1, :] = positions[pl.ds(pairs[slot], 1), :]
            bodies[slot:slot + 1, :] = bodies_in[pl.ds(pairs[slot], 1), :]
        weight_rows(spots, weights)
        for slot in range(8):
            pair_partials(slot, pairs[slot], grid_rows, weights, spread.at[slot % 2], product.at[slot % 2], partial)
        sums = group_sums(partial, bodies)
        for slot in range(8):
            results[pl.ds(pairs[slot], 1), :] = sums[slot:slot + 1]
        return carry

    lax.fori_loop(0, (count + 7) // 8, group, 0)


def pair_scratch(width):
    return [
        pltpu.VMEM((8, width), F32),
        pltpu.VMEM((72, width), F32),
        pltpu.VMEM((2, 2 * GRID, width // 3), F32),
        pltpu.VMEM((2, GRID * GRID, width), BF16),
        pltpu.VMEM((8, 64, 128), F32),
        pltpu.VMEM((8, width), F32),
    ]


def own_kernel(first_s, sdf_s, live_s, first, sdf, listed, poses, grids, body_table, knots, offsets,
               results, positions, bodies_out, pose_pairs, targets, order_out,
               grid_rows, own_order, padded, pieces, table, sems, *scratch):
    chunks = sems.shape[0]
    wide = grids.shape[1] // chunks
    copies = []
    for index in range(chunks):
        part = pl.ds(index * wide, wide)
        copy = pltpu.make_async_copy(grids.at[:, part], table.at[:, part], sems.at[index])
        copy.start()
        copies.append(copy)
    pairs, width = positions.shape
    grains = body_table.shape[0]
    signs = parity_signs()

    def sort_pair(pair, counts):
        own, ghost = counts
        live = live_s[pair]
        near = jnp.where(sdf_s[pair] < grains, 1, 0)
        own_order[own] = pair
        order_out[ghost] = pair
        return own + live * near, ghost + live * (1 - near)

    own, ghost = lax.fori_loop(0, pairs, sort_pair, (0, 0))
    own_last = own_order[jnp.maximum(own - 1, 0)]
    ghost_last = order_out[jnp.maximum(ghost - 1, 0)]
    for extra in range(8):
        own_order[own + extra] = own_last
        order_out[ghost + extra] = ghost_last
    order_out[143] = ghost

    results[...] = jnp.zeros_like(results)
    positions[...] = knots[...].astype(F32) + offsets[...]

    def copy_body(pair, carry):
        bodies_out[pl.ds(pair, 1), :] = body_table[pl.ds(first_s[pair], 1), :]
        return carry

    lax.fori_loop(0, pairs, copy_body, 0, unroll=8)

    rows = lax.broadcasted_iota(jnp.int32, (grains, pairs), 0)
    first_hot = jnp.where(rows == first[...], 1.0, 0.0).astype(BF16)
    sdf_hot32 = jnp.where(rows == sdf[...], 1.0, 0.0)
    pose_pieces(poses, pieces, padded)
    pose_pairs[0:48, :] = dot(pieces[...], first_hot)
    pose_pairs[48:96, :] = dot(pieces[...], sdf_hot32.astype(BF16))
    hot = sdf_hot32.T.astype(BF16)
    for cell in range(GRID):
        if cell % (GRID // chunks) == 0:
            copies[cell // (GRID // chunks)].wait()
        part = slice(cell * GRID * GRID, cell * GRID * GRID + GRID * GRID)
        spread_rows(grid_rows, cell, dot(hot, table[:, part]))

    targets[...] = jnp.zeros_like(targets)
    for base, op in ((0, "A"), (128, "B"), (256, "C"), (288, "AC"), (320, "BC"), (384, "D"), (416, "BD"), (448, "AD")):
        targets[base:base + 32, :] = one_hot_rows(listed_column(listed, signs, op), grains)

    pair_loop(own, own_order, grid_rows, positions, bodies_out, results, scratch)


def own_pairs(first, sdf, live, listed, poses, grids, body_table, knots, offsets):
    pairs, width = knots.shape
    grains, cells = grids.shape
    vmem = pl.BlockSpec(memory_space=pltpu.VMEM)
    smem = pl.BlockSpec(memory_space=pltpu.SMEM)
    return pl.pallas_call(
        own_kernel,
        out_shape=[
            jax.ShapeDtypeStruct((pairs, 128), F32),
            jax.ShapeDtypeStruct((pairs, width), F32),
            jax.ShapeDtypeStruct((pairs, width), F32),
            jax.ShapeDtypeStruct((96, pairs), F32),
            jax.ShapeDtypeStruct((512, grains), BF16),
            jax.ShapeDtypeStruct((144,), jnp.int32),
        ],
        in_specs=[smem] * 3 + [vmem] * 4 + [pl.BlockSpec(memory_space=pl.ANY)] + [vmem] * 3,
        out_specs=[vmem] * 5 + [smem],
        scratch_shapes=[
            pltpu.VMEM((2, pairs * GRID, 128), F32),
            pltpu.SMEM((144,), jnp.int32),
            pltpu.VMEM((16, grains), F32),
            pltpu.VMEM((48, grains), BF16),
            pltpu.VMEM((grains, cells), BF16),
            pltpu.SemaphoreType.DMA((4,)),
        ] + pair_scratch(width),
        cost_estimate=pl.CostEstimate(flops=6 * 10**9, bytes_accessed=16 * 10**6, transcendentals=0),
        name="own_pairs",
    )(first, sdf, live, first.reshape(1, pairs), sdf.reshape(1, pairs), listed, poses, grids, body_table, knots, offsets)


def joined(value, base):
    return value[base:base + 12] + value[base + 16:base + 28] + value[base + 32:base + 44]


def ghost_kernel(order, first, sdf, own_results, positions, bodies_in, pose_pairs, *refs):
    payloads = refs[:8]
    own_sum, load_a, load_b, load_c, load_d = refs[8:13]
    ghosts, results, grid_rows = refs[13:16]
    scratch = refs[16:]
    pairs = positions.shape[0]
    grains = own_sum.shape[1]
    cells = GRID * GRID * GRID
    signs = parity_signs()
    for index in range(8):
        ghosts[32 * index:32 * index + 32, :] = payloads[index][...]

    row = sdf[...]
    ghost = row - grains
    direction = jnp.right_shift(ghost, 5)
    slot = jnp.bitwise_and(ghost, 31)
    cell = direction + jnp.where(direction >= 4, 1, 0)
    third = jnp.where(cell >= 6, 2, jnp.where(cell >= 3, 1, 0))
    row_step = (third - 1) * signs[0]
    col_step = (cell - 3 * third - 1) * signs[1]
    buffer_row = jnp.zeros_like(row)
    place = jnp.zeros_like(row)
    bases = {"A": 0, "AC": 32, "AD": 64, "B": 128, "BD": 160, "BC": 192, "C": 256, "D": 384}
    for index, op in enumerate(OPS):
        row_want, col_want = steps_of(op)
        match = (row_step == row_want) & (col_step == col_want)
        buffer_row = jnp.where(match, 32 * index, buffer_row)
        place = jnp.where(match, bases[op], place)
    buffer_row = jnp.where(ghost >= 0, buffer_row + slot, -1)
    place = jnp.where(ghost >= 0, place + slot, -1)

    slot_rows = lax.broadcasted_iota(jnp.int32, (256, pairs), 0)
    slot_hot = jnp.where(slot_rows == buffer_row, 1.0, 0.0)
    hot = slot_hot.T.astype(BF16)
    for index in range(GRID):
        part = slice(index * GRID * GRID, index * GRID * GRID + GRID * GRID)
        spread_rows(grid_rows, index, dot(hot, ghosts[:, part]))
    ghost_pose = dot(ghosts[:, cells:].astype(F32).T.astype(BF16), slot_hot.astype(BF16))

    results[...] = own_results[...]
    pair_loop(order[143], order, grid_rows, positions, bodies_in, results, scratch)

    sums = results[...].T
    pose_first = joined(pose_pairs[...], 0)
    pose_second = joined(pose_pairs[...], 48) + joined(ghost_pose, 0)
    take = lambda value, index: value[index:index + 1]
    total = [take(sums, m) * STIFFNESS for m in range(3)]
    moment = [[take(sums, 3 + 3 * l + m) * STIFFNESS for m in range(3)] for l in range(3)]
    turn_1 = [[take(pose_first, 3 + 3 * i + j) for j in range(3)] for i in range(3)]
    turn_2 = [[take(pose_second, 3 + 3 * i + j) for j in range(3)] for i in range(3)]
    apart = [take(pose_first, i) - take(pose_second, i) for i in range(3)]
    force = [turn_2[i][0] * total[0] + turn_2[i][1] * total[1] + turn_2[i][2] * total[2] for i in range(3)]
    half = [[turn_1[j][0] * moment[0][m] + turn_1[j][1] * moment[1][m] + turn_1[j][2] * moment[2][m]
             for m in range(3)] for j in range(3)]
    outer = [[half[j][0] * turn_2[k][0] + half[j][1] * turn_2[k][1] + half[j][2] * turn_2[k][2]
              for k in range(3)] for j in range(3)]
    first_moment = [outer[1][2] - outer[2][1], outer[2][0] - outer[0][2], outer[0][1] - outer[1][0]]
    crossed = [apart[1] * force[2] - apart[2] * force[1], apart[2] * force[0] - apart[0] * force[2],
               apart[0] * force[1] - apart[1] * force[0]]
    second_moment = [-(crossed[i] + first_moment[i]) for i in range(3)]
    zero = jnp.zeros_like(force[0])
    loads_1 = jnp.concatenate(force + first_moment + [zero, zero], axis=0)
    loads_2 = jnp.concatenate([-value for value in force] + second_moment + [zero, zero], axis=0)
    loads_1 = jnp.concatenate(split3_rows(loads_1), axis=0).astype(BF16)
    loads_2 = jnp.concatenate(split3_rows(loads_2), axis=0).astype(BF16)
    rows = lax.broadcasted_iota(jnp.int32, (grains, pairs), 0)
    first_hot = jnp.where(rows == first[...], 1.0, 0.0).astype(BF16)
    own_hot = jnp.where(rows == row, 1.0, 0.0).astype(BF16)
    place_hot = jnp.where(rows == place, 1.0, 0.0).astype(BF16)
    near = dot(loads_1, first_hot, NT) + dot(loads_2, own_hot, NT)
    own_sum[...] = near[0:8] + near[8:16] + near[16:24]
    far = dot(loads_2, place_hot, NT)
    far = far[0:8] + far[8:16] + far[16:24]
    for index, out in enumerate((load_a, load_b, load_c, load_d)):
        out[...] = far[:, 128 * index:128 * index + 128]


def split3_rows(value):
    return [piece.astype(F32) for piece in split3(value)]


def ghost_pairs(order, first, sdf, own_results, positions, bodies, pose_pairs, payloads, grains):
    pairs, width = positions.shape
    vmem = pl.BlockSpec(memory_space=pltpu.VMEM)
    smem = pl.BlockSpec(memory_space=pltpu.SMEM)
    load = jax.ShapeDtypeStruct((8, 128), F32)
    return pl.pallas_call(
        ghost_kernel,
        out_shape=[jax.ShapeDtypeStruct((8, grains), F32)] + [load] * 4,
        in_specs=[smem] + [vmem] * 14,
        out_specs=[vmem] * 5,
        scratch_shapes=[
            pltpu.VMEM((256, payloads[0].shape[1]), BF16),
            pltpu.VMEM((pairs, 128), F32),
            pltpu.VMEM((2, pairs * GRID, 128), F32),
        ] + pair_scratch(width),
        name="ghost_pairs",
    )(order, first.reshape(1, pairs), sdf.reshape(1, pairs), own_results, positions, bodies, pose_pairs, *payloads)


def return_kernel(own_sum, load_a, load_b, load_c, load_d, targets, out):
    loads = jnp.concatenate([load_a[...], load_b[...], load_c[...], load_d[...]], axis=1)
    pieces = jnp.concatenate(split3_rows(loads), axis=0).astype(BF16)
    added = dot(pieces, targets[...])
    total = own_sum[...] + (added[0:8] + added[8:16] + added[16:24])
    out[...] = total[0:6]


def return_loads(own_sum, loads, targets):
    vmem = pl.BlockSpec(memory_space=pltpu.VMEM)
    return pl.pallas_call(
        return_kernel,
        out_shape=jax.ShapeDtypeStruct((6, own_sum.shape[1]), F32),
        in_specs=[vmem] * 6,
        out_specs=vmem,
        name="return_loads",
    )(own_sum, *loads, targets)


def swapped(block, op, rows, cols):
    route = []
    row_step, col_step = steps_of(op)
    for r in range(rows):
        for c in range(cols):
            to_r = (r + row_step * (1 - 2 * (r % 2))) % rows
            to_c = (c + col_step * (1 - 2 * (c % 2))) % cols
            route.append((r * cols + c, to_r * cols + to_c))
    return lax.ppermute(block, ("row", "col"), route)


def local(rows, cols, sdf_grids, grain_poses, surface_nodes, send_list, pair_first, pair_sdf, pair_pose, pair_live,
          knot_cells, offsets):
    grains = sdf_grids.shape[0]
    listed = send_list.reshape(8, send_list.shape[3])
    swap = lambda block, op: swapped(block, op, rows, cols)
    packed = pack(listed, grain_poses, sdf_grids)
    payloads = [swap(block, op) for block, op in zip(packed, OPS)]
    results, positions, bodies, pose_pairs, targets, order = own_pairs(
        pair_first, pair_sdf, pair_live, listed, grain_poses, sdf_grids, surface_nodes, knot_cells, offsets)
    own_sum, load_a, load_b, load_c, load_d = ghost_pairs(
        order, pair_first, pair_sdf, results, positions, bodies, pose_pairs, payloads, grains)
    back_a, back_b = swap(load_a, "A"), swap(load_b, "B")
    lanes = lax.broadcasted_iota(jnp.int32, load_a.shape, 1)
    send_c = jnp.where(lanes < 32, load_c, jnp.where(lanes < 64, back_a, back_b))
    send_d = jnp.where(lanes < 32, load_d, jnp.where(lanes < 64, back_b, back_a))
    back_c, back_d = swap(send_c, "C"), swap(send_d, "D")
    return return_loads(own_sum, (back_a, back_b, back_c, back_d), targets)


def solution(mesh):
    in_specs = (
        P(("row", "col"), None),
        P(None, ("row", "col")),
        P(("row", "col"), None),
        P("row", "col", None, None),
        P(("row", "col")),
        P(("row", "col")),
        P(("row", "col")),
        P(("row", "col")),
        P(("row", "col"), None),
        P(("row", "col"), None),
    )
    out_specs = P(None, ("row", "col"))
    body = functools.partial(local, mesh.shape["row"], mesh.shape["col"])
    return jax.shard_map(body, mesh=mesh, in_specs=in_specs, out_specs=out_specs, check_vma=False)
```

```python
import functools

import jax
import jax.numpy as jnp
from jax import lax
from jax.experimental import pallas as pl
from jax.experimental.pallas import tpu as pltpu
from jax.sharding import PartitionSpec as P

GRID = 16
STIFFNESS = 0.25
OPS = ("C", "D", "AC", "AD", "BC", "BD", "A", "B")
F32 = jnp.float32
BF16 = jnp.bfloat16
NN = (((1,), (0,)), ((), ()))
NT = (((1,), (1,)), ((), ()))


def steps_of(op):
    row = 1 if "A" in op else (-1 if "B" in op else 0)
    col = 1 if "C" in op else (-1 if "D" in op else 0)
    return row, col


def direction_of(row_step, col_step):
    cell = (row_step + 1) * 3 + col_step + 1
    return cell - (cell > 4).astype(jnp.int32)


def parity_signs():
    return 1 - 2 * (lax.axis_index("row") & 1), 1 - 2 * (lax.axis_index("col") & 1)


def split3(value):
    high = value.astype(BF16)
    rest = value - high.astype(F32)
    middle = rest.astype(BF16)
    low = (rest - middle.astype(F32)).astype(BF16)
    return high, middle, low


def dot(left, right, dims=NN):
    return lax.dot_general(left, right, dims, preferred_element_type=F32)


def listed_column(listed, signs, op):
    row_step, col_step = steps_of(op)
    direction = direction_of(row_step * signs[0], col_step * signs[1])
    row = listed[pl.ds(direction, 1), :].astype(F32)
    size = row.shape[1]
    eye = lax.broadcasted_iota(jnp.int32, (size, size), 0) == lax.broadcasted_iota(jnp.int32, (size, size), 1)
    return jnp.sum(jnp.where(eye, row, 0.0), axis=1, keepdims=True)


def one_hot_rows(column, width):
    lanes = lax.broadcasted_iota(jnp.int32, (column.shape[0], width), 1).astype(F32)
    return jnp.where(lanes == column, 1.0, 0.0).astype(BF16)


def pose_pieces(poses, pieces, padded):
    padded[...] = jnp.zeros_like(padded)
    padded[0:12, :] = poses[...]
    for index, piece in enumerate(split3(padded[...])):
        pieces[16 * index:16 * index + 16, :] = piece


def pack_kernel(listed_in, poses_in, grids, *refs):
    outs, table = refs[:8], refs[8]
    listed, poses, hot, padded, pieces, sems, small_sems = refs[9:]
    chunks = sems.shape[0]
    grains, cells = grids.shape
    width = cells // chunks
    small = [pltpu.make_async_copy(listed_in, listed, small_sems.at[0]),
             pltpu.make_async_copy(poses_in, poses, small_sems.at[1])]
    for copy in small:
        copy.start()
    copies = []
    for index in range(chunks):
        part = pl.ds(index * width, width)
        copy = pltpu.make_async_copy(grids.at[:, part], table.at[:, part], sems.at[index])
        copy.start()
        copies.append(copy)
    signs = parity_signs()
    for copy in small:
        copy.wait()
    for index, op in enumerate(OPS):
        hot[32 * index:32 * index + 32, :] = one_hot_rows(listed_column(listed, signs, op), grains)
    pieces[...] = jnp.zeros_like(pieces)
    pose_pieces(poses, pieces, padded)
    rows = dot(hot[...], pieces[...], NT).astype(BF16)
    for index in range(8):
        outs[index][:, cells:] = rows[32 * index:32 * index + 32]
    for step in range(chunks):
        copies[step].wait()
        part = slice(step * width, step * width + width)
        rows = dot(hot[...], table[:, part]).astype(BF16)
        for index in range(8):
            outs[index][:, part] = rows[32 * index:32 * index + 32]


def pack(listed, poses, grids):
    grains, cells = grids.shape
    vmem = pl.BlockSpec(memory_space=pltpu.VMEM)
    *payloads, table = pl.pallas_call(
        pack_kernel,
        out_shape=[jax.ShapeDtypeStruct((32, cells + 128), BF16)] * 8 + [jax.ShapeDtypeStruct(grids.shape, BF16)],
        in_specs=[pl.BlockSpec(memory_space=pltpu.HBM)] * 3,
        out_specs=[vmem] * 9,
        scratch_shapes=[
            pltpu.VMEM(listed.shape, jnp.int32),
            pltpu.VMEM(poses.shape, F32),
            pltpu.VMEM((256, grains), BF16),
            pltpu.VMEM((16, grains), F32),
            pltpu.VMEM((128, grains), BF16),
            pltpu.SemaphoreType.DMA((8,)),
            pltpu.SemaphoreType.DMA((2,)),
        ],
        compiler_params=pltpu.CompilerParams(vmem_limit_bytes=16 * 2**20),
        name="pack",
    )(*(pltpu.with_memory_space_constraint(value, pltpu.HBM) for value in (listed, poses, grids)))
    return payloads, table


def weight_rows(cells, parts, weights):
    nodes = parts.shape[1] // 3
    u = parts[...]
    v = 1.0 - u
    u2 = u * u
    u3 = u2 * u
    v2 = v * v
    rows = [
        v2 * v * (1.0 / 6.0),
        0.5 * u3 - u2 + 2.0 / 3.0,
        0.5 * (u2 + u - u3) + 1.0 / 6.0,
        u3 * (1.0 / 6.0),
        -0.5 * v2,
        1.5 * u2 - 2.0 * u,
        -1.5 * u2 + u + 0.5,
        0.5 * u2,
    ]
    weights[0:8, :] = cells[...].astype(F32) - 1.0
    for index, row in enumerate(rows):
        part = slice(8 * index + 8, 8 * index + 16)
        weights[part, 0:nodes] = row[:, 0:nodes].astype(BF16).astype(F32)
        weights[part, nodes:] = row[:, nodes:]


def spline(weights, slot, axis):
    nodes = weights.shape[1] // 3
    row = lambda index: weights[8 * index + slot:8 * index + slot + 1, axis * nodes:axis * nodes + nodes]
    cells = lax.broadcasted_iota(jnp.int32, (GRID, nodes), 0).astype(F32)
    place = cells - row(0)
    at = [place == float(index) for index in range(4)]
    result = []
    for first in (1, 5):
        value = jnp.where(at[3], row(first + 3), 0.0)
        for index in (2, 1, 0):
            value = jnp.where(at[index], row(first + index), value)
        result.append(value)
    return result


def spread_rows(grid_rows, cell, values):
    for half in range(2):
        pairs = values.shape[0]
        grid_rows[half, cell * pairs:cell * pairs + pairs, :] = values[:, 128 * half:128 * half + 128]


def pair_partials(slot, pair, grid_rows, weights, spread, product, partial):
    nodes = weights.shape[1] // 3
    cube_rows = pl.ds(pair, GRID, stride=grid_rows.shape[1] // GRID)
    cube = jnp.concatenate([grid_rows[half, cube_rows, :].astype(BF16) for half in range(2)], axis=1)
    spread[0:GRID, :], spread[GRID:2 * GRID, :] = spline(weights, slot, 1)
    basis_z, slope_z = spline(weights, slot, 2)
    for cell in range(GRID):
        plain = spread[cell:cell + 1, :]
        tilt = spread[GRID + cell:GRID + cell + 1, :]
        rows = slice(cell * GRID, cell * GRID + GRID)
        product[rows, 0:nodes] = (plain * basis_z).astype(BF16)
        product[rows, nodes:2 * nodes] = (tilt * basis_z).astype(BF16)
        product[rows, 2 * nodes:3 * nodes] = (plain * slope_z).astype(BF16)
    basis_x, slope_x = spline(weights, slot, 0)
    sums = dot(cube, product[...])
    plain = sums[:, 0:nodes]
    for index, (weight, term) in enumerate(
        ((basis_x, plain), (slope_x, plain), (basis_x, sums[:, nodes:2 * nodes]), (basis_x, sums[:, 2 * nodes:]))
    ):
        both = weight * term
        both = both[0:8] + both[8:16]
        for half in range(2):
            partial[2 * index + half, slot * 8:slot * 8 + 8, :] = both[:, 128 * half:128 * half + 128]


def group_sums(partial, bodies):
    nodes = 2 * partial.shape[2]
    totals = []
    for index in range(4):
        halves = []
        for half in range(2):
            parts = [partial[2 * index + half, pl.ds(part, 8, stride=8), :] for part in range(8)]
            while len(parts) > 1:
                parts = [left + right for left, right in zip(parts[::2], parts[1::2])]
            halves.append(parts[0])
        totals.append(jnp.concatenate(halves, axis=1))
    push = jnp.maximum(-totals[0], 0.0)
    force = [push * totals[1], push * totals[2], push * totals[3]]
    lanes = lax.broadcasted_iota(jnp.int32, (8, 128), 1)
    result = jnp.zeros((8, 128), F32)
    for m in range(3):
        result = jnp.where(lanes == m, jnp.sum(force[m], axis=1, keepdims=True), result)
        for l in range(3):
            product = bodies[:, l * nodes:l * nodes + nodes] * force[m]
            result = jnp.where(lanes == 3 + 3 * l + m, jnp.sum(product, axis=1, keepdims=True), result)
    return result


def pair_loop(count, order, first, grid_rows, knots, offsets, body_table, results, scratch):
    cells, parts, weights, spread, product, partial, bodies = scratch

    def group(index, carry):
        pairs = [order[index * 8 + slot] for slot in range(8)]
        for slot in range(8):
            cells[slot:slot + 1, :] = knots[pl.ds(pairs[slot], 1), :]
            parts[slot:slot + 1, :] = offsets[pl.ds(pairs[slot], 1), :]
            bodies[slot:slot + 1, :] = body_table[pl.ds(first[pairs[slot]], 1), :]
        weight_rows(cells, parts, weights)
        for slot in range(8):
            pair_partials(slot, pairs[slot], grid_rows, weights, spread.at[slot % 2], product.at[slot % 2], partial)
        sums = group_sums(partial, bodies)
        for slot in range(8):
            results[pl.ds(pairs[slot], 1), :] = sums[slot:slot + 1]
        return carry

    lax.fori_loop(0, (count + 7) // 8, group, 0)


def pair_scratch(width):
    return [
        pltpu.VMEM((8, width), jnp.int32),
        pltpu.VMEM((8, width), F32),
        pltpu.VMEM((72, width), F32),
        pltpu.VMEM((2, 2 * GRID, width // 3), F32),
        pltpu.VMEM((2, GRID * GRID, width), BF16),
        pltpu.VMEM((8, 64, 128), F32),
        pltpu.VMEM((8, width), F32),
    ]


def own_kernel(first_s, sdf_s, live_s, first, sdf, poses, grids, body_table, knots, offsets,
               results, pose_pairs, order_out, grid_rows, own_order, padded, pieces, *scratch):
    pairs = knots.shape[0]
    grains = grids.shape[0]

    def sort_pair(pair, counts):
        own, ghost = counts
        live = live_s[pair]
        near = jnp.where(sdf_s[pair] < grains, live, 0)
        own_order[own] = pair
        order_out[ghost] = pair
        return own + near, ghost + live - near

    own, ghost = lax.fori_loop(0, pairs, sort_pair, (0, 0), unroll=8)
    own_last = own_order[jnp.maximum(own - 1, 0)]
    ghost_last = order_out[jnp.maximum(ghost - 1, 0)]
    for extra in range(8):
        own_order[own + extra] = own_last
        order_out[ghost + extra] = ghost_last
    order_out[143] = ghost

    results[...] = jnp.zeros_like(results)
    rows = lax.broadcasted_iota(jnp.int32, (grains, pairs), 0)
    first_hot = jnp.where(rows == first[...], 1.0, 0.0).astype(BF16)
    sdf_hot32 = jnp.where(rows == sdf[...], 1.0, 0.0)
    pose_pieces(poses, pieces, padded)
    pose_pairs[0:48, :] = dot(pieces[...], first_hot)
    pose_pairs[48:96, :] = dot(pieces[...], sdf_hot32.astype(BF16))
    hot = sdf_hot32.T.astype(BF16)
    spread_table(grid_rows, hot, grids)
    pair_loop(own, own_order, first_s, grid_rows, knots, offsets, body_table, results, scratch)


def spread_table(grid_rows, hot, table):
    square = GRID * GRID
    wide = 4 * square
    for index in range(4):
        values = dot(hot, table[:, index * wide:index * wide + wide])
        for inner in range(4):
            spread_rows(grid_rows, index * 4 + inner, values[:, inner * square:inner * square + square])


def own_pairs(first, sdf, live, poses, grids, body_table, knots, offsets):
    pairs, width = knots.shape
    grains, cells = grids.shape
    vmem = pl.BlockSpec(memory_space=pltpu.VMEM)
    smem = pl.BlockSpec(memory_space=pltpu.SMEM)
    return pl.pallas_call(
        own_kernel,
        out_shape=[
            jax.ShapeDtypeStruct((pairs, 128), F32),
            jax.ShapeDtypeStruct((96, pairs), F32),
            jax.ShapeDtypeStruct((144,), jnp.int32),
        ],
        in_specs=[smem] * 3 + [vmem] * 7,
        out_specs=[vmem] * 2 + [smem],
        scratch_shapes=[
            pltpu.VMEM((2, pairs * GRID, 128), F32),
            pltpu.SMEM((144,), jnp.int32),
            pltpu.VMEM((16, grains), F32),
            pltpu.VMEM((48, grains), BF16),
        ] + pair_scratch(width),
        cost_estimate=pl.CostEstimate(flops=6 * 10**9, bytes_accessed=16 * 10**6, transcendentals=0),
        compiler_params=pltpu.CompilerParams(vmem_limit_bytes=16 * 2**20),
        name="own_pairs",
    )(first, sdf, live, first.reshape(1, pairs), sdf.reshape(1, pairs), poses, grids, body_table, knots, offsets)


def joined(value, base):
    return value[base:base + 12] + value[base + 16:base + 28] + value[base + 32:base + 44]


def ghost_kernel(order, first_s, first, sdf, own_results, knots, offsets, body_table, pose_pairs, *refs):
    payloads = refs[:8]
    own_sum, load_a, load_b, load_c, load_d = refs[8:13]
    ghosts, results, grid_rows = refs[13:16]
    scratch = refs[16:]
    pairs = knots.shape[0]
    grains = own_sum.shape[1]
    cells = GRID * GRID * GRID
    signs = parity_signs()
    for index in range(8):
        ghosts[32 * index:32 * index + 32, :] = payloads[index][...]

    row = sdf[...]
    ghost = row - grains
    direction = jnp.right_shift(ghost, 5)
    slot = jnp.bitwise_and(ghost, 31)
    cell = direction + jnp.where(direction >= 4, 1, 0)
    third = jnp.where(cell >= 6, 2, jnp.where(cell >= 3, 1, 0))
    row_step = (third - 1) * signs[0]
    col_step = (cell - 3 * third - 1) * signs[1]
    buffer_row = jnp.zeros_like(row)
    place = jnp.zeros_like(row)
    bases = {"A": 0, "AC": 32, "AD": 64, "B": 128, "BD": 160, "BC": 192, "C": 256, "D": 384}
    for index, op in enumerate(OPS):
        row_want, col_want = steps_of(op)
        match = (row_step == row_want) & (col_step == col_want)
        buffer_row = jnp.where(match, 32 * index, buffer_row)
        place = jnp.where(match, bases[op], place)
    buffer_row = jnp.where(ghost >= 0, buffer_row + slot, -1)
    place = jnp.where(ghost >= 0, place + slot, -1)

    slot_rows = lax.broadcasted_iota(jnp.int32, (256, pairs), 0)
    slot_hot = jnp.where(slot_rows == buffer_row, 1.0, 0.0)
    hot = slot_hot.T.astype(BF16)
    spread_table(grid_rows, hot, ghosts)
    ghost_pose = dot(ghosts[:, cells:].astype(F32).T.astype(BF16), slot_hot.astype(BF16))

    results[...] = own_results[...]
    pair_loop(order[143], order, first_s, grid_rows, knots, offsets, body_table, results, scratch)

    sums = results[...].T
    pose_first = joined(pose_pairs[...], 0)
    pose_second = joined(pose_pairs[...], 48) + joined(ghost_pose, 0)
    take = lambda value, index: value[index:index + 1]
    total = [take(sums, m) * STIFFNESS for m in range(3)]
    moment = [[take(sums, 3 + 3 * l + m) * STIFFNESS for m in range(3)] for l in range(3)]
    turn_1 = [[take(pose_first, 3 + 3 * i + j) for j in range(3)] for i in range(3)]
    turn_2 = [[take(pose_second, 3 + 3 * i + j) for j in range(3)] for i in range(3)]
    apart = [take(pose_first, i) - take(pose_second, i) for i in range(3)]
    force = [turn_2[i][0] * total[0] + turn_2[i][1] * total[1] + turn_2[i][2] * total[2] for i in range(3)]
    half = [[turn_1[j][0] * moment[0][m] + turn_1[j][1] * moment[1][m] + turn_1[j][2] * moment[2][m]
             for m in range(3)] for j in range(3)]
    outer = [[half[j][0] * turn_2[k][0] + half[j][1] * turn_2[k][1] + half[j][2] * turn_2[k][2]
              for k in range(3)] for j in range(3)]
    first_moment = [outer[1][2] - outer[2][1], outer[2][0] - outer[0][2], outer[0][1] - outer[1][0]]
    crossed = [apart[1] * force[2] - apart[2] * force[1], apart[2] * force[0] - apart[0] * force[2],
               apart[0] * force[1] - apart[1] * force[0]]
    second_moment = [-(crossed[i] + first_moment[i]) for i in range(3)]
    zero = jnp.zeros_like(force[0])
    loads_1 = jnp.concatenate(force + first_moment + [zero, zero], axis=0)
    loads_2 = jnp.concatenate([-value for value in force] + second_moment + [zero, zero], axis=0)
    loads_1 = jnp.concatenate(split3_rows(loads_1), axis=0).astype(BF16)
    loads_2 = jnp.concatenate(split3_rows(loads_2), axis=0).astype(BF16)
    rows = lax.broadcasted_iota(jnp.int32, (grains, pairs), 0)
    first_hot = jnp.where(rows == first[...], 1.0, 0.0).astype(BF16)
    own_hot = jnp.where(rows == row, 1.0, 0.0).astype(BF16)
    place_hot = jnp.where(rows == place, 1.0, 0.0).astype(BF16)
    near = dot(loads_1, first_hot, NT) + dot(loads_2, own_hot, NT)
    own_sum[...] = near[0:8] + near[8:16] + near[16:24]
    far = dot(loads_2, place_hot, NT)
    far = far[0:8] + far[8:16] + far[16:24]
    for index, out in enumerate((load_a, load_b, load_c, load_d)):
        out[...] = far[:, 128 * index:128 * index + 128]


def split3_rows(value):
    return [piece.astype(F32) for piece in split3(value)]


def ghost_pairs(order, first, sdf, own_results, knots, offsets, body_table, pose_pairs, payloads):
    pairs, width = knots.shape
    grains = body_table.shape[0]
    vmem = pl.BlockSpec(memory_space=pltpu.VMEM)
    smem = pl.BlockSpec(memory_space=pltpu.SMEM)
    load = jax.ShapeDtypeStruct((8, 128), F32)
    return pl.pallas_call(
        ghost_kernel,
        out_shape=[jax.ShapeDtypeStruct((8, grains), F32)] + [load] * 4,
        in_specs=[smem] * 2 + [vmem] * 15,
        out_specs=[vmem] * 5,
        scratch_shapes=[
            pltpu.VMEM((256, payloads[0].shape[1]), BF16),
            pltpu.VMEM((pairs, 128), F32),
            pltpu.VMEM((2, pairs * GRID, 128), F32),
        ] + pair_scratch(width),
        cost_estimate=pl.CostEstimate(flops=6 * 10**9, bytes_accessed=16 * 10**6, transcendentals=0),
        compiler_params=pltpu.CompilerParams(vmem_limit_bytes=16 * 2**20),
        name="ghost_pairs",
    )(order, first, first.reshape(1, pairs), sdf.reshape(1, pairs), own_results, knots, offsets, body_table, pose_pairs,
      *payloads)


def return_kernel(listed, own_sum, load_a, load_b, load_c, load_d, out, targets):
    signs = parity_signs()
    grains = own_sum.shape[1]
    targets[...] = jnp.zeros_like(targets)
    for base, op in ((0, "A"), (128, "B"), (256, "C"), (288, "AC"), (320, "BC"), (384, "D"), (416, "BD"), (448, "AD")):
        targets[base:base + 32, :] = one_hot_rows(listed_column(listed, signs, op), grains)
    loads = jnp.concatenate([load_a[...], load_b[...], load_c[...], load_d[...]], axis=1)
    pieces = jnp.concatenate(split3_rows(loads), axis=0).astype(BF16)
    added = dot(pieces, targets[...])
    total = own_sum[...] + (added[0:8] + added[8:16] + added[16:24])
    out[...] = total[0:6]


def return_loads(listed, own_sum, loads):
    vmem = pl.BlockSpec(memory_space=pltpu.VMEM)
    return pl.pallas_call(
        return_kernel,
        out_shape=jax.ShapeDtypeStruct((6, own_sum.shape[1]), F32),
        in_specs=[vmem] * 6,
        out_specs=vmem,
        scratch_shapes=[pltpu.VMEM((512, own_sum.shape[1]), BF16)],
        compiler_params=pltpu.CompilerParams(vmem_limit_bytes=4 * 2**20),
        name="return_loads",
    )(listed, own_sum, *loads)


def swapped(block, op, rows, cols):
    route = []
    row_step, col_step = steps_of(op)
    for r in range(rows):
        for c in range(cols):
            to_r = (r + row_step * (1 - 2 * (r % 2))) % rows
            to_c = (c + col_step * (1 - 2 * (c % 2))) % cols
            route.append((r * cols + c, to_r * cols + to_c))
    return lax.ppermute(block, ("row", "col"), route)


def local(rows, cols, sdf_grids, grain_poses, surface_nodes, send_list, pair_first, pair_sdf, pair_pose, pair_live,
          knot_cells, offsets):
    listed = send_list.reshape(8, send_list.shape[3])
    swap = lambda block, op: swapped(block, op, rows, cols)
    packed, table = pack(listed, grain_poses, sdf_grids)
    payloads = [swap(block, op) for block, op in zip(packed, OPS)]
    results, pose_pairs, order = own_pairs(
        pair_first, pair_sdf, pair_live, grain_poses, table, surface_nodes, knot_cells, offsets)
    own_sum, load_a, load_b, load_c, load_d = ghost_pairs(
        order, pair_first, pair_sdf, results, knot_cells, offsets, surface_nodes, pose_pairs, payloads)
    back_a, back_b = swap(load_a, "A"), swap(load_b, "B")
    lanes = lax.broadcasted_iota(jnp.int32, load_a.shape, 1)
    send_c = jnp.where(lanes < 32, load_c, jnp.where(lanes < 64, back_a, back_b))
    send_d = jnp.where(lanes < 32, load_d, jnp.where(lanes < 64, back_b, back_a))
    back_c, back_d = swap(send_c, "C"), swap(send_d, "D")
    return return_loads(listed, own_sum, (back_a, back_b, back_c, back_d))


def solution(mesh):
    in_specs = (
        P(("row", "col"), None),
        P(None, ("row", "col")),
        P(("row", "col"), None),
        P("row", "col", None, None),
        P(("row", "col")),
        P(("row", "col")),
        P(("row", "col")),
        P(("row", "col")),
        P(("row", "col"), None),
        P(("row", "col"), None),
    )
    out_specs = P(None, ("row", "col"))
    body = functools.partial(local, mesh.shape["row"], mesh.shape["col"])
    return jax.shard_map(body, mesh=mesh, in_specs=in_specs, out_specs=out_specs, check_vma=False)
```

```python
import functools

import jax
import jax.numpy as jnp
from jax import lax
from jax.experimental import pallas as pl
from jax.experimental.pallas import tpu as pltpu
from jax.sharding import PartitionSpec as P

GRID = 16
STIFFNESS = 0.25
OPS = ("C", "D", "AC", "AD", "BC", "BD", "A", "B")
F32 = jnp.float32
BF16 = jnp.bfloat16
NN = (((1,), (0,)), ((), ()))
NT = (((1,), (1,)), ((), ()))


def steps_of(op):
    row = 1 if "A" in op else (-1 if "B" in op else 0)
    col = 1 if "C" in op else (-1 if "D" in op else 0)
    return row, col


def direction_of(row_step, col_step):
    cell = (row_step + 1) * 3 + col_step + 1
    return cell - (cell > 4).astype(jnp.int32)


def parity_signs():
    return 1 - 2 * (lax.axis_index("row") & 1), 1 - 2 * (lax.axis_index("col") & 1)


def split3(value):
    high = value.astype(BF16)
    rest = value - high.astype(F32)
    middle = rest.astype(BF16)
    low = (rest - middle.astype(F32)).astype(BF16)
    return high, middle, low


def dot(left, right, dims=NN):
    return lax.dot_general(left, right, dims, preferred_element_type=F32)


def listed_column(listed, signs, op):
    row_step, col_step = steps_of(op)
    direction = direction_of(row_step * signs[0], col_step * signs[1])
    row = listed[pl.ds(direction, 1), :].astype(F32)
    size = row.shape[1]
    eye = lax.broadcasted_iota(jnp.int32, (size, size), 0) == lax.broadcasted_iota(jnp.int32, (size, size), 1)
    return jnp.sum(jnp.where(eye, row, 0.0), axis=1, keepdims=True)


def one_hot_rows(column, width):
    lanes = lax.broadcasted_iota(jnp.int32, (column.shape[0], width), 1).astype(F32)
    return jnp.where(lanes == column, 1.0, 0.0).astype(BF16)


def pose_pieces(poses, pieces, padded):
    padded[...] = jnp.zeros_like(padded)
    padded[0:12, :] = poses[...]
    for index, piece in enumerate(split3(padded[...])):
        pieces[16 * index:16 * index + 16, :] = piece


def pack_kernel(listed_in, poses_in, grids, *refs):
    outs, table = refs[:8], refs[8]
    listed, poses, hot, padded, pieces, sems, small_sems = refs[9:]
    chunks = sems.shape[0]
    grains, cells = grids.shape
    width = cells // chunks
    small = [pltpu.make_async_copy(listed_in, listed, small_sems.at[0]),
             pltpu.make_async_copy(poses_in, poses, small_sems.at[1])]
    for copy in small:
        copy.start()
    copies = []
    for index in range(chunks):
        part = pl.ds(index * width, width)
        copy = pltpu.make_async_copy(grids.at[:, part], table.at[:, part], sems.at[index])
        copy.start()
        copies.append(copy)
    signs = parity_signs()
    for copy in small:
        copy.wait()
    for index, op in enumerate(OPS):
        hot[32 * index:32 * index + 32, :] = one_hot_rows(listed_column(listed, signs, op), grains)
    pieces[...] = jnp.zeros_like(pieces)
    pose_pieces(poses, pieces, padded)
    rows = dot(hot[...], pieces[...], NT).astype(BF16)
    for index in range(8):
        outs[index][:, cells:] = rows[32 * index:32 * index + 32]
    for step in range(chunks):
        copies[step].wait()
        part = slice(step * width, step * width + width)
        rows = dot(hot[...], table[:, part]).astype(BF16)
        for index in range(8):
            outs[index][:, part] = rows[32 * index:32 * index + 32]


def pack(listed, poses, grids):
    grains, cells = grids.shape
    vmem = pl.BlockSpec(memory_space=pltpu.VMEM)
    *payloads, table = pl.pallas_call(
        pack_kernel,
        out_shape=[jax.ShapeDtypeStruct((32, cells + 128), BF16)] * 8 + [jax.ShapeDtypeStruct(grids.shape, BF16)],
        in_specs=[pl.BlockSpec(memory_space=pltpu.HBM)] * 3,
        out_specs=[vmem] * 9,
        scratch_shapes=[
            pltpu.VMEM(listed.shape, jnp.int32),
            pltpu.VMEM(poses.shape, F32),
            pltpu.VMEM((256, grains), BF16),
            pltpu.VMEM((16, grains), F32),
            pltpu.VMEM((128, grains), BF16),
            pltpu.SemaphoreType.DMA((2,)),
            pltpu.SemaphoreType.DMA((2,)),
        ],
        compiler_params=pltpu.CompilerParams(vmem_limit_bytes=16 * 2**20),
        name="pack",
    )(*(pltpu.with_memory_space_constraint(value, pltpu.HBM) for value in (listed, poses, grids)))
    return payloads, table


def weight_rows(cells, parts, weights):
    nodes = parts.shape[1] // 3
    u = parts[...]
    v = 1.0 - u
    u2 = u * u
    u3 = u2 * u
    v2 = v * v
    rows = [
        v2 * v * (1.0 / 6.0),
        0.5 * u3 - u2 + 2.0 / 3.0,
        0.5 * (u2 + u - u3) + 1.0 / 6.0,
        u3 * (1.0 / 6.0),
        -0.5 * v2,
        1.5 * u2 - 2.0 * u,
        -1.5 * u2 + u + 0.5,
        0.5 * u2,
    ]
    weights[0:8, :] = cells[...].astype(F32) - 1.0
    for index, row in enumerate(rows):
        part = slice(8 * index + 8, 8 * index + 16)
        weights[part, 0:nodes] = row[:, 0:nodes].astype(BF16).astype(F32)
        weights[part, nodes:] = row[:, nodes:]


def spline(weights, slot, axis):
    nodes = weights.shape[1] // 3
    row = lambda index: weights[8 * index + slot:8 * index + slot + 1, axis * nodes:axis * nodes + nodes]
    cells = lax.broadcasted_iota(jnp.int32, (GRID, nodes), 0).astype(F32)
    place = cells - row(0)
    at = [place == float(index) for index in range(4)]
    result = []
    for first in (1, 5):
        value = jnp.where(at[3], row(first + 3), 0.0)
        for index in (2, 1, 0):
            value = jnp.where(at[index], row(first + index), value)
        result.append(value)
    return result


def spread_rows(grid_rows, cell, values):
    for half in range(2):
        pairs = values.shape[0]
        grid_rows[half, cell * pairs:cell * pairs + pairs, :] = values[:, 128 * half:128 * half + 128]


def pair_partials(slot, pair, grid_rows, weights, spread, product, partial):
    nodes = weights.shape[1] // 3
    cube_rows = pl.ds(pair, GRID, stride=grid_rows.shape[1] // GRID)
    cube = jnp.concatenate([grid_rows[half, cube_rows, :].astype(BF16) for half in range(2)], axis=1)
    spread[0:GRID, :], spread[GRID:2 * GRID, :] = spline(weights, slot, 1)
    basis_z, slope_z = spline(weights, slot, 2)
    for cell in range(GRID):
        plain = spread[cell:cell + 1, :]
        tilt = spread[GRID + cell:GRID + cell + 1, :]
        rows = slice(cell * GRID, cell * GRID + GRID)
        product[rows, 0:nodes] = (plain * basis_z).astype(BF16)
        product[rows, nodes:2 * nodes] = (tilt * basis_z).astype(BF16)
        product[rows, 2 * nodes:3 * nodes] = (plain * slope_z).astype(BF16)
    basis_x, slope_x = spline(weights, slot, 0)
    sums = dot(cube, product[...])
    plain = sums[:, 0:nodes]
    for index, (weight, term) in enumerate(
        ((basis_x, plain), (slope_x, plain), (basis_x, sums[:, nodes:2 * nodes]), (basis_x, sums[:, 2 * nodes:]))
    ):
        both = weight * term
        both = both[0:8] + both[8:16]
        for half in range(2):
            partial[2 * index + half, slot * 8:slot * 8 + 8, :] = both[:, 128 * half:128 * half + 128]


def group_sums(partial, bodies):
    nodes = 2 * partial.shape[2]
    totals = []
    for index in range(4):
        halves = []
        for half in range(2):
            parts = [partial[2 * index + half, pl.ds(part, 8, stride=8), :] for part in range(8)]
            while len(parts) > 1:
                parts = [left + right for left, right in zip(parts[::2], parts[1::2])]
            halves.append(parts[0])
        totals.append(jnp.concatenate(halves, axis=1))
    push = jnp.maximum(-totals[0], 0.0)
    force = [push * totals[1], push * totals[2], push * totals[3]]
    lanes = lax.broadcasted_iota(jnp.int32, (8, 128), 1)
    result = jnp.zeros((8, 128), F32)
    for m in range(3):
        result = jnp.where(lanes == m, jnp.sum(force[m], axis=1, keepdims=True), result)
        for l in range(3):
            product = bodies[:, l * nodes:l * nodes + nodes] * force[m]
            result = jnp.where(lanes == 3 + 3 * l + m, jnp.sum(product, axis=1, keepdims=True), result)
    return result


def pair_loop(count, order, first, grid_rows, knots, offsets, body_table, results, scratch):
    cells, parts, weights, spread, product, partial, bodies = scratch

    def group(index, carry):
        pairs = [order[index * 8 + slot] for slot in range(8)]
        for slot in range(8):
            cells[slot:slot + 1, :] = knots[pl.ds(pairs[slot], 1), :]
            parts[slot:slot + 1, :] = offsets[pl.ds(pairs[slot], 1), :]
            bodies[slot:slot + 1, :] = body_table[pl.ds(first[pairs[slot]], 1), :]
        weight_rows(cells, parts, weights)
        for slot in range(8):
            pair_partials(slot, pairs[slot], grid_rows, weights, spread.at[slot % 2], product.at[slot % 2], partial)
        sums = group_sums(partial, bodies)
        for slot in range(8):
            results[pl.ds(pairs[slot], 1), :] = sums[slot:slot + 1]
        return carry

    lax.fori_loop(0, (count + 7) // 8, group, 0)


def pair_scratch(width):
    return [
        pltpu.VMEM((8, width), jnp.int32),
        pltpu.VMEM((8, width), F32),
        pltpu.VMEM((72, width), F32),
        pltpu.VMEM((2, 2 * GRID, width // 3), F32),
        pltpu.VMEM((2, GRID * GRID, width), BF16),
        pltpu.VMEM((8, 64, 128), F32),
        pltpu.VMEM((8, width), F32),
    ]


def own_kernel(first_s, sdf_s, live_s, first, sdf, poses, grids, body_table, knots, offsets,
               results, pose_pairs, order_out, grid_rows, own_order, padded, pieces, *scratch):
    pairs = knots.shape[0]
    grains = grids.shape[0]

    def sort_pair(pair, counts):
        own, ghost = counts
        live = live_s[pair]
        near = jnp.where(sdf_s[pair] < grains, live, 0)
        own_order[own] = pair
        order_out[ghost] = pair
        return own + near, ghost + live - near

    own, ghost = lax.fori_loop(0, pairs, sort_pair, (0, 0), unroll=8)
    own_last = own_order[jnp.maximum(own - 1, 0)]
    ghost_last = order_out[jnp.maximum(ghost - 1, 0)]
    for extra in range(8):
        own_order[own + extra] = own_last
        order_out[ghost + extra] = ghost_last
    order_out[143] = ghost

    results[...] = jnp.zeros_like(results)
    rows = lax.broadcasted_iota(jnp.int32, (grains, pairs), 0)
    first_hot = jnp.where(rows == first[...], 1.0, 0.0).astype(BF16)
    sdf_hot32 = jnp.where(rows == sdf[...], 1.0, 0.0)
    pose_pieces(poses, pieces, padded)
    pose_pairs[0:48, :] = dot(pieces[...], first_hot)
    pose_pairs[48:96, :] = dot(pieces[...], sdf_hot32.astype(BF16))
    hot = sdf_hot32.T.astype(BF16)
    spread_table(grid_rows, hot, lambda part: grids[:, part])
    pair_loop(own, own_order, first_s, grid_rows, knots, offsets, body_table, results, scratch)


def spread_table(grid_rows, hot, part_of):
    square = GRID * GRID
    wide = 4 * square
    for index in range(4):
        values = dot(hot, part_of(slice(index * wide, index * wide + wide)))
        for inner in range(4):
            spread_rows(grid_rows, index * 4 + inner, values[:, inner * square:inner * square + square])


def own_pairs(first, sdf, live, poses, grids, body_table, knots, offsets):
    pairs, width = knots.shape
    grains, cells = grids.shape
    vmem = pl.BlockSpec(memory_space=pltpu.VMEM)
    smem = pl.BlockSpec(memory_space=pltpu.SMEM)
    return pl.pallas_call(
        own_kernel,
        out_shape=[
            jax.ShapeDtypeStruct((pairs, 128), F32),
            jax.ShapeDtypeStruct((96, pairs), F32),
            jax.ShapeDtypeStruct((144,), jnp.int32),
        ],
        in_specs=[smem] * 3 + [vmem] * 7,
        out_specs=[vmem] * 2 + [smem],
        scratch_shapes=[
            pltpu.VMEM((2, pairs * GRID, 128), F32),
            pltpu.SMEM((144,), jnp.int32),
            pltpu.VMEM((16, grains), F32),
            pltpu.VMEM((48, grains), BF16),
        ] + pair_scratch(width),
        cost_estimate=pl.CostEstimate(flops=6 * 10**9, bytes_accessed=16 * 10**6, transcendentals=0),
        compiler_params=pltpu.CompilerParams(vmem_limit_bytes=16 * 2**20),
        name="own_pairs",
    )(first, sdf, live, first.reshape(1, pairs), sdf.reshape(1, pairs), poses, grids, body_table, knots, offsets)


def joined(value, base):
    return value[base:base + 12] + value[base + 16:base + 28] + value[base + 32:base + 44]


def ghost_kernel(order, first_s, first, sdf, own_results, knots, offsets, body_table, pose_pairs, *refs):
    payloads = refs[:8]
    own_sum, load_a, load_b, load_c, load_d = refs[8:13]
    results, grid_rows = refs[13:15]
    scratch = refs[15:]
    pairs = knots.shape[0]
    grains = own_sum.shape[1]
    cells = GRID * GRID * GRID
    signs = parity_signs()
    row = sdf[...]
    ghost = row - grains
    direction = jnp.right_shift(ghost, 5)
    slot = jnp.bitwise_and(ghost, 31)
    cell = direction + jnp.where(direction >= 4, 1, 0)
    third = jnp.where(cell >= 6, 2, jnp.where(cell >= 3, 1, 0))
    row_step = (third - 1) * signs[0]
    col_step = (cell - 3 * third - 1) * signs[1]
    buffer_row = jnp.zeros_like(row)
    place = jnp.zeros_like(row)
    bases = {"A": 0, "AC": 32, "AD": 64, "B": 128, "BD": 160, "BC": 192, "C": 256, "D": 384}
    for index, op in enumerate(OPS):
        row_want, col_want = steps_of(op)
        match = (row_step == row_want) & (col_step == col_want)
        buffer_row = jnp.where(match, 32 * index, buffer_row)
        place = jnp.where(match, bases[op], place)
    buffer_row = jnp.where(ghost >= 0, buffer_row + slot, -1)
    place = jnp.where(ghost >= 0, place + slot, -1)

    slot_rows = lax.broadcasted_iota(jnp.int32, (256, pairs), 0)
    slot_hot = jnp.where(slot_rows == buffer_row, 1.0, 0.0)
    hot = slot_hot.T.astype(BF16)
    joint = lambda part: jnp.concatenate([payload[:, part] for payload in payloads], axis=0)
    spread_table(grid_rows, hot, joint)
    ghost_pose = dot(joint(slice(cells, cells + 128)).astype(F32).T.astype(BF16), slot_hot.astype(BF16))

    results[...] = own_results[...]
    pair_loop(order[143], order, first_s, grid_rows, knots, offsets, body_table, results, scratch)

    sums = results[...].T
    pose_first = joined(pose_pairs[...], 0)
    pose_second = joined(pose_pairs[...], 48) + joined(ghost_pose, 0)
    take = lambda value, index: value[index:index + 1]
    total = [take(sums, m) * STIFFNESS for m in range(3)]
    moment = [[take(sums, 3 + 3 * l + m) * STIFFNESS for m in range(3)] for l in range(3)]
    turn_1 = [[take(pose_first, 3 + 3 * i + j) for j in range(3)] for i in range(3)]
    turn_2 = [[take(pose_second, 3 + 3 * i + j) for j in range(3)] for i in range(3)]
    apart = [take(pose_first, i) - take(pose_second, i) for i in range(3)]
    force = [turn_2[i][0] * total[0] + turn_2[i][1] * total[1] + turn_2[i][2] * total[2] for i in range(3)]
    half = [[turn_1[j][0] * moment[0][m] + turn_1[j][1] * moment[1][m] + turn_1[j][2] * moment[2][m]
             for m in range(3)] for j in range(3)]
    outer = [[half[j][0] * turn_2[k][0] + half[j][1] * turn_2[k][1] + half[j][2] * turn_2[k][2]
              for k in range(3)] for j in range(3)]
    first_moment = [outer[1][2] - outer[2][1], outer[2][0] - outer[0][2], outer[0][1] - outer[1][0]]
    crossed = [apart[1] * force[2] - apart[2] * force[1], apart[2] * force[0] - apart[0] * force[2],
               apart[0] * force[1] - apart[1] * force[0]]
    second_moment = [-(crossed[i] + first_moment[i]) for i in range(3)]
    zero = jnp.zeros_like(force[0])
    loads_1 = jnp.concatenate(force + first_moment + [zero, zero], axis=0)
    loads_2 = jnp.concatenate([-value for value in force] + second_moment + [zero, zero], axis=0)
    loads_1 = jnp.concatenate(split3_rows(loads_1), axis=0).astype(BF16)
    loads_2 = jnp.concatenate(split3_rows(loads_2), axis=0).astype(BF16)
    rows = lax.broadcasted_iota(jnp.int32, (grains, pairs), 0)
    first_hot = jnp.where(rows == first[...], 1.0, 0.0).astype(BF16)
    own_hot = jnp.where(rows == row, 1.0, 0.0).astype(BF16)
    place_hot = jnp.where(rows == place, 1.0, 0.0).astype(BF16)
    near = dot(loads_1, first_hot, NT) + dot(loads_2, own_hot, NT)
    own_sum[...] = near[0:8] + near[8:16] + near[16:24]
    far = dot(loads_2, place_hot, NT)
    far = far[0:8] + far[8:16] + far[16:24]
    for index, out in enumerate((load_a, load_b, load_c, load_d)):
        out[...] = far[:, 128 * index:128 * index + 128]


def split3_rows(value):
    return [piece.astype(F32) for piece in split3(value)]


def ghost_pairs(order, first, sdf, own_results, knots, offsets, body_table, pose_pairs, payloads):
    pairs, width = knots.shape
    grains = body_table.shape[0]
    vmem = pl.BlockSpec(memory_space=pltpu.VMEM)
    smem = pl.BlockSpec(memory_space=pltpu.SMEM)
    load = jax.ShapeDtypeStruct((8, 128), F32)
    return pl.pallas_call(
        ghost_kernel,
        out_shape=[jax.ShapeDtypeStruct((8, grains), F32)] + [load] * 4,
        in_specs=[smem] * 2 + [vmem] * 15,
        out_specs=[vmem] * 5,
        scratch_shapes=[
            pltpu.VMEM((pairs, 128), F32),
            pltpu.VMEM((2, pairs * GRID, 128), F32),
        ] + pair_scratch(width),
        cost_estimate=pl.CostEstimate(flops=6 * 10**9, bytes_accessed=16 * 10**6, transcendentals=0),
        compiler_params=pltpu.CompilerParams(vmem_limit_bytes=16 * 2**20),
        name="ghost_pairs",
    )(order, first, first.reshape(1, pairs), sdf.reshape(1, pairs), own_results, knots, offsets, body_table, pose_pairs,
      *payloads)


def return_kernel(listed, own_sum, load_a, load_b, load_c, load_d, out, targets):
    signs = parity_signs()
    grains = own_sum.shape[1]
    targets[...] = jnp.zeros_like(targets)
    for base, op in ((0, "A"), (128, "B"), (256, "C"), (288, "AC"), (320, "BC"), (384, "D"), (416, "BD"), (448, "AD")):
        targets[base:base + 32, :] = one_hot_rows(listed_column(listed, signs, op), grains)
    loads = jnp.concatenate([load_a[...], load_b[...], load_c[...], load_d[...]], axis=1)
    pieces = jnp.concatenate(split3_rows(loads), axis=0).astype(BF16)
    added = dot(pieces, targets[...])
    total = own_sum[...] + (added[0:8] + added[8:16] + added[16:24])
    out[...] = total[0:6]


def return_loads(listed, own_sum, loads):
    vmem = pl.BlockSpec(memory_space=pltpu.VMEM)
    return pl.pallas_call(
        return_kernel,
        out_shape=jax.ShapeDtypeStruct((6, own_sum.shape[1]), F32),
        in_specs=[vmem] * 6,
        out_specs=vmem,
        scratch_shapes=[pltpu.VMEM((512, own_sum.shape[1]), BF16)],
        compiler_params=pltpu.CompilerParams(vmem_limit_bytes=4 * 2**20),
        name="return_loads",
    )(listed, own_sum, *loads)


def swapped(block, op, rows, cols):
    route = []
    row_step, col_step = steps_of(op)
    for r in range(rows):
        for c in range(cols):
            to_r = (r + row_step * (1 - 2 * (r % 2))) % rows
            to_c = (c + col_step * (1 - 2 * (c % 2))) % cols
            route.append((r * cols + c, to_r * cols + to_c))
    return lax.ppermute(block, ("row", "col"), route)


def local(rows, cols, sdf_grids, grain_poses, surface_nodes, send_list, pair_first, pair_sdf, pair_pose, pair_live,
          knot_cells, offsets):
    listed = send_list.reshape(8, send_list.shape[3])
    swap = lambda block, op: swapped(block, op, rows, cols)
    packed, table = pack(listed, grain_poses, sdf_grids)
    payloads = [swap(block, op) for block, op in zip(packed, OPS)]
    results, pose_pairs, order = own_pairs(
        pair_first, pair_sdf, pair_live, grain_poses, table, surface_nodes, knot_cells, offsets)
    own_sum, load_a, load_b, load_c, load_d = ghost_pairs(
        order, pair_first, pair_sdf, results, knot_cells, offsets, surface_nodes, pose_pairs, payloads)
    back_a, back_b = swap(load_a, "A"), swap(load_b, "B")
    lanes = lax.broadcasted_iota(jnp.int32, load_a.shape, 1)
    send_c = jnp.where(lanes < 32, load_c, jnp.where(lanes < 64, back_a, back_b))
    send_d = jnp.where(lanes < 32, load_d, jnp.where(lanes < 64, back_b, back_a))
    back_c, back_d = swap(send_c, "C"), swap(send_d, "D")
    return return_loads(listed, own_sum, (back_a, back_b, back_c, back_d))


def solution(mesh):
    in_specs = (
        P(("row", "col"), None),
        P(None, ("row", "col")),
        P(("row", "col"), None),
        P("row", "col", None, None),
        P(("row", "col")),
        P(("row", "col")),
        P(("row", "col")),
        P(("row", "col")),
        P(("row", "col"), None),
        P(("row", "col"), None),
    )
    out_specs = P(None, ("row", "col"))
    body = functools.partial(local, mesh.shape["row"], mesh.shape["col"])
    return jax.shard_map(body, mesh=mesh, in_specs=in_specs, out_specs=out_specs, check_vma=False)
```

```python
import functools

import jax
import jax.numpy as jnp
from jax import lax
from jax.experimental import pallas as pl
from jax.experimental.pallas import tpu as pltpu
from jax.sharding import PartitionSpec as P

GRID = 16
STIFFNESS = 0.25
OPS = ("C", "D", "AC", "AD", "BC", "BD", "A", "B")
F32 = jnp.float32
BF16 = jnp.bfloat16
NN = (((1,), (0,)), ((), ()))
NT = (((1,), (1,)), ((), ()))


def steps_of(op):
    row = 1 if "A" in op else (-1 if "B" in op else 0)
    col = 1 if "C" in op else (-1 if "D" in op else 0)
    return row, col


def direction_of(row_step, col_step):
    cell = (row_step + 1) * 3 + col_step + 1
    return cell - (cell > 4).astype(jnp.int32)


def parity_signs():
    return 1 - 2 * (lax.axis_index("row") & 1), 1 - 2 * (lax.axis_index("col") & 1)


def split3(value):
    high = value.astype(BF16)
    rest = value - high.astype(F32)
    middle = rest.astype(BF16)
    low = (rest - middle.astype(F32)).astype(BF16)
    return high, middle, low


def dot(left, right, dims=NN):
    return lax.dot_general(left, right, dims, preferred_element_type=F32)


def listed_column(listed, signs, op):
    row_step, col_step = steps_of(op)
    direction = direction_of(row_step * signs[0], col_step * signs[1])
    row = listed[pl.ds(direction, 1), :].astype(F32)
    size = row.shape[1]
    eye = lax.broadcasted_iota(jnp.int32, (size, size), 0) == lax.broadcasted_iota(jnp.int32, (size, size), 1)
    return jnp.sum(jnp.where(eye, row, 0.0), axis=1, keepdims=True)


def one_hot_rows(column, width):
    lanes = lax.broadcasted_iota(jnp.int32, (column.shape[0], width), 1).astype(F32)
    return jnp.where(lanes == column, 1.0, 0.0).astype(BF16)


def pose_pieces(poses, pieces, padded):
    padded[...] = jnp.zeros_like(padded)
    padded[0:12, :] = poses[...]
    for index, piece in enumerate(split3(padded[...])):
        pieces[16 * index:16 * index + 16, :] = piece


def pack_kernel(listed_in, poses_in, grids, *refs):
    outs, table = refs[:8], refs[8]
    listed, poses, hot, padded, pieces, sems, small_sems = refs[9:]
    chunks = sems.shape[0]
    grains, cells = grids.shape
    width = cells // chunks
    small = [pltpu.make_async_copy(listed_in, listed, small_sems.at[0]),
             pltpu.make_async_copy(poses_in, poses, small_sems.at[1])]
    for copy in small:
        copy.start()
    copies = []
    for index in range(chunks):
        part = pl.ds(index * width, width)
        copy = pltpu.make_async_copy(grids.at[:, part], table.at[:, part], sems.at[index])
        copy.start()
        copies.append(copy)
    signs = parity_signs()
    for copy in small:
        copy.wait()
    for index, op in enumerate(OPS):
        hot[32 * index:32 * index + 32, :] = one_hot_rows(listed_column(listed, signs, op), grains)
    pieces[...] = jnp.zeros_like(pieces)
    pose_pieces(poses, pieces, padded)
    rows = dot(hot[...], pieces[...], NT).astype(BF16)
    for index in range(8):
        outs[index][:, cells:] = rows[32 * index:32 * index + 32]
    for step in range(chunks):
        copies[step].wait()
        part = slice(step * width, step * width + width)
        rows = dot(hot[...], table[:, part]).astype(BF16)
        for index in range(8):
            outs[index][:, part] = rows[32 * index:32 * index + 32]


def pack(listed, poses, grids):
    grains, cells = grids.shape
    vmem = pl.BlockSpec(memory_space=pltpu.VMEM)
    *payloads, table = pl.pallas_call(
        pack_kernel,
        out_shape=[jax.ShapeDtypeStruct((32, cells + 128), BF16)] * 8 + [jax.ShapeDtypeStruct(grids.shape, BF16)],
        in_specs=[pl.BlockSpec(memory_space=pltpu.HBM)] * 3,
        out_specs=[vmem] * 9,
        scratch_shapes=[
            pltpu.VMEM(listed.shape, jnp.int32),
            pltpu.VMEM(poses.shape, F32),
            pltpu.VMEM((256, grains), BF16),
            pltpu.VMEM((16, grains), F32),
            pltpu.VMEM((128, grains), BF16),
            pltpu.SemaphoreType.DMA((2,)),
            pltpu.SemaphoreType.DMA((2,)),
        ],
        compiler_params=pltpu.CompilerParams(vmem_limit_bytes=16 * 2**20),
        name="pack",
    )(*(pltpu.with_memory_space_constraint(value, pltpu.HBM) for value in (listed, poses, grids)))
    return payloads, table


def weight_rows(cells, parts, weights):
    nodes = parts.shape[1] // 3
    u = parts[...]
    v = 1.0 - u
    u2 = u * u
    u3 = u2 * u
    v2 = v * v
    rows = [
        v2 * v * (1.0 / 6.0),
        0.5 * u3 - u2 + 2.0 / 3.0,
        0.5 * (u2 + u - u3) + 1.0 / 6.0,
        u3 * (1.0 / 6.0),
        -0.5 * v2,
        1.5 * u2 - 2.0 * u,
        -1.5 * u2 + u + 0.5,
        0.5 * u2,
    ]
    weights[0:8, :] = cells[...].astype(F32) - 1.0
    for index, row in enumerate(rows):
        part = slice(8 * index + 8, 8 * index + 16)
        weights[part, 0:nodes] = row[:, 0:nodes].astype(BF16).astype(F32)
        weights[part, nodes:] = row[:, nodes:]


def spline(weights, slot, axis):
    nodes = weights.shape[1] // 3
    row = lambda index: weights[8 * index + slot:8 * index + slot + 1, axis * nodes:axis * nodes + nodes]
    cells = lax.broadcasted_iota(jnp.int32, (GRID, nodes), 0).astype(F32)
    place = cells - row(0)
    at = [place == float(index) for index in range(4)]
    result = []
    for first in (1, 5):
        value = jnp.where(at[3], row(first + 3), 0.0)
        for index in (2, 1, 0):
            value = jnp.where(at[index], row(first + index), value)
        result.append(value)
    return result


def spread_rows(grid_rows, cell, values):
    for half in range(2):
        pairs = values.shape[0]
        grid_rows[half, cell * pairs:cell * pairs + pairs, :] = values[:, 128 * half:128 * half + 128]


def pair_partials(slot, pair, grid_rows, weights, spread, product, partial):
    nodes = weights.shape[1] // 3
    cube_rows = pl.ds(pair, GRID, stride=grid_rows.shape[1] // GRID)
    cube = jnp.concatenate([grid_rows[half, cube_rows, :].astype(BF16) for half in range(2)], axis=1)
    spread[0:GRID, :], spread[GRID:2 * GRID, :] = spline(weights, slot, 1)
    basis_z, slope_z = spline(weights, slot, 2)
    for cell in range(GRID):
        plain = spread[cell:cell + 1, :]
        tilt = spread[GRID + cell:GRID + cell + 1, :]
        rows = slice(cell * GRID, cell * GRID + GRID)
        product[rows, 0:nodes] = (plain * basis_z).astype(BF16)
        product[rows, nodes:2 * nodes] = (tilt * basis_z).astype(BF16)
        product[rows, 2 * nodes:3 * nodes] = (plain * slope_z).astype(BF16)
    basis_x, slope_x = spline(weights, slot, 0)
    sums = dot(cube, product[...])
    plain = sums[:, 0:nodes]
    for index, (weight, term) in enumerate(
        ((basis_x, plain), (slope_x, plain), (basis_x, sums[:, nodes:2 * nodes]), (basis_x, sums[:, 2 * nodes:]))
    ):
        both = weight * term
        both = both[0:8] + both[8:16]
        for half in range(2):
            partial[2 * index + half, slot * 8:slot * 8 + 8, :] = both[:, 128 * half:128 * half + 128]


def group_sums(partial, bodies):
    nodes = bodies.shape[1] // 3
    totals = []
    for index in range(4):
        halves = []
        for half in range(2):
            parts = [partial[2 * index + half, pl.ds(part, 8, stride=8), :] for part in range(8)]
            while len(parts) > 1:
                parts = [left + right for left, right in zip(parts[::2], parts[1::2])]
            halves.append(parts[0])
        totals.append(jnp.concatenate(halves, axis=1))
    push = jnp.maximum(-totals[0], 0.0)
    force = [push * totals[1], push * totals[2], push * totals[3]]
    lanes = lax.broadcasted_iota(jnp.int32, (8, 128), 1)
    result = jnp.zeros((8, 128), F32)
    for m in range(3):
        result = jnp.where(lanes == m, jnp.sum(force[m], axis=1, keepdims=True), result)
        for l in range(3):
            product = bodies[:, l * nodes:l * nodes + nodes] * force[m]
            result = jnp.where(lanes == 3 + 3 * l + m, jnp.sum(product, axis=1, keepdims=True), result)
    return result


def pair_loop(count, order, first, grid_rows, knots, offsets, body_table, results, scratch):
    cells, parts, weights, spread, product, partial, bodies = scratch
    groups = (count + 7) // 8

    def two_of(step):
        return 2 * step, jnp.minimum(2 * step + 1, groups - 1)

    def prepare(step, carry):
        for lane, index in enumerate(two_of(step)):
            for slot in range(8):
                pair = order[index * 8 + slot]
                cells[lane, slot:slot + 1, :] = knots[pl.ds(pair, 1), :]
                parts[lane, slot:slot + 1, :] = offsets[pl.ds(pair, 1), :]
        for lane, index in enumerate(two_of(step)):
            weight_rows(cells.at[lane], parts.at[lane], weights.at[index])
        return carry

    def finish(index):
        pairs = [order[index * 8 + slot] for slot in range(8)]
        for slot in range(8):
            bodies[slot:slot + 1, :] = body_table[pl.ds(first[pairs[slot]], 1), :]
        sums = group_sums(partial.at[index], bodies)
        for slot in range(8):
            results[pl.ds(pairs[slot], 1), :] = sums[slot:slot + 1]

    def compute(index, carry):
        finish(jnp.maximum(index - 1, 0))
        for slot in range(8):
            pair_partials(slot, order[index * 8 + slot], grid_rows, weights.at[index], spread.at[slot % 2],
                          product.at[slot % 2], partial.at[index])
        return carry

    lax.fori_loop(0, (groups + 1) // 2, prepare, 0)
    lax.fori_loop(0, groups, compute, 0)

    @pl.when(groups > 0)
    def _():
        finish(groups - 1)


def pair_scratch(width, pairs):
    groups = pairs // 8
    return [
        pltpu.VMEM((2, 8, width), jnp.int32),
        pltpu.VMEM((2, 8, width), F32),
        pltpu.VMEM((groups, 72, width), F32),
        pltpu.VMEM((2, 2 * GRID, width // 3), F32),
        pltpu.VMEM((2, GRID * GRID, width), BF16),
        pltpu.VMEM((groups, 8, 64, 128), F32),
        pltpu.VMEM((8, width), F32),
    ]


def own_kernel(first_s, sdf_s, live_s, first, sdf, poses, grids, body_table, knots, offsets,
               results, pose_pairs, order_out, grid_rows, own_order, padded, pieces, *scratch):
    pairs = knots.shape[0]
    grains = grids.shape[0]

    def sort_pair(pair, counts):
        own, ghost = counts
        live = live_s[pair]
        near = jnp.where(sdf_s[pair] < grains, live, 0)
        own_order[own] = pair
        order_out[ghost] = pair
        return own + near, ghost + live - near

    own, ghost = lax.fori_loop(0, pairs, sort_pair, (0, 0), unroll=8)
    own_last = own_order[jnp.maximum(own - 1, 0)]
    ghost_last = order_out[jnp.maximum(ghost - 1, 0)]
    for extra in range(8):
        own_order[own + extra] = own_last
        order_out[ghost + extra] = ghost_last
    order_out[143] = ghost

    results[...] = jnp.zeros_like(results)
    rows = lax.broadcasted_iota(jnp.int32, (grains, pairs), 0)
    first_hot = jnp.where(rows == first[...], 1.0, 0.0).astype(BF16)
    sdf_hot32 = jnp.where(rows == sdf[...], 1.0, 0.0)
    pose_pieces(poses, pieces, padded)
    pose_pairs[0:48, :] = dot(pieces[...], first_hot)
    pose_pairs[48:96, :] = dot(pieces[...], sdf_hot32.astype(BF16))
    hot = sdf_hot32.T.astype(BF16)
    spread_table(grid_rows, hot, lambda part: grids[:, part])
    pair_loop(own, own_order, first_s, grid_rows, knots, offsets, body_table, results, scratch)


def spread_table(grid_rows, hot, part_of):
    square = GRID * GRID
    wide = 4 * square
    for index in range(4):
        values = dot(hot, part_of(slice(index * wide, index * wide + wide)))
        for inner in range(4):
            spread_rows(grid_rows, index * 4 + inner, values[:, inner * square:inner * square + square])


def own_pairs(first, sdf, live, poses, grids, body_table, knots, offsets):
    pairs, width = knots.shape
    grains, cells = grids.shape
    vmem = pl.BlockSpec(memory_space=pltpu.VMEM)
    smem = pl.BlockSpec(memory_space=pltpu.SMEM)
    return pl.pallas_call(
        own_kernel,
        out_shape=[
            jax.ShapeDtypeStruct((pairs, 128), F32),
            jax.ShapeDtypeStruct((96, pairs), F32),
            jax.ShapeDtypeStruct((144,), jnp.int32),
        ],
        in_specs=[smem] * 3 + [vmem] * 7,
        out_specs=[vmem] * 2 + [smem],
        scratch_shapes=[
            pltpu.VMEM((2, pairs * GRID, 128), F32),
            pltpu.SMEM((144,), jnp.int32),
            pltpu.VMEM((16, grains), F32),
            pltpu.VMEM((48, grains), BF16),
        ] + pair_scratch(width, pairs),
        cost_estimate=pl.CostEstimate(flops=6 * 10**9, bytes_accessed=16 * 10**6, transcendentals=0),
        compiler_params=pltpu.CompilerParams(vmem_limit_bytes=24 * 2**20),
        name="own_pairs",
    )(first, sdf, live, first.reshape(1, pairs), sdf.reshape(1, pairs), poses, grids, body_table, knots, offsets)


def joined(value, base):
    return value[base:base + 12] + value[base + 16:base + 28] + value[base + 32:base + 44]


def ghost_kernel(order, first_s, first, sdf, own_results, knots, offsets, body_table, pose_pairs, *refs):
    payloads = refs[:8]
    own_sum, load_a, load_b, load_c, load_d = refs[8:13]
    results, grid_rows = refs[13:15]
    scratch = refs[15:]
    pairs = knots.shape[0]
    grains = own_sum.shape[1]
    cells = GRID * GRID * GRID
    signs = parity_signs()
    row = sdf[...]
    ghost = row - grains
    direction = jnp.right_shift(ghost, 5)
    slot = jnp.bitwise_and(ghost, 31)
    cell = direction + jnp.where(direction >= 4, 1, 0)
    third = jnp.where(cell >= 6, 2, jnp.where(cell >= 3, 1, 0))
    row_step = (third - 1) * signs[0]
    col_step = (cell - 3 * third - 1) * signs[1]
    buffer_row = jnp.zeros_like(row)
    place = jnp.zeros_like(row)
    bases = {"A": 0, "AC": 32, "AD": 64, "B": 128, "BD": 160, "BC": 192, "C": 256, "D": 384}
    for index, op in enumerate(OPS):
        row_want, col_want = steps_of(op)
        match = (row_step == row_want) & (col_step == col_want)
        buffer_row = jnp.where(match, 32 * index, buffer_row)
        place = jnp.where(match, bases[op], place)
    buffer_row = jnp.where(ghost >= 0, buffer_row + slot, -1)
    place = jnp.where(ghost >= 0, place + slot, -1)

    slot_rows = lax.broadcasted_iota(jnp.int32, (256, pairs), 0)
    slot_hot = jnp.where(slot_rows == buffer_row, 1.0, 0.0)
    hot = slot_hot.T.astype(BF16)
    joint = lambda part: jnp.concatenate([payload[:, part] for payload in payloads], axis=0)
    spread_table(grid_rows, hot, joint)
    ghost_pose = dot(joint(slice(cells, cells + 128)).astype(F32).T.astype(BF16), slot_hot.astype(BF16))

    results[...] = own_results[...]
    pair_loop(order[143], order, first_s, grid_rows, knots, offsets, body_table, results, scratch)

    sums = results[...].T
    pose_first = joined(pose_pairs[...], 0)
    pose_second = joined(pose_pairs[...], 48) + joined(ghost_pose, 0)
    take = lambda value, index: value[index:index + 1]
    total = [take(sums, m) * STIFFNESS for m in range(3)]
    moment = [[take(sums, 3 + 3 * l + m) * STIFFNESS for m in range(3)] for l in range(3)]
    turn_1 = [[take(pose_first, 3 + 3 * i + j) for j in range(3)] for i in range(3)]
    turn_2 = [[take(pose_second, 3 + 3 * i + j) for j in range(3)] for i in range(3)]
    apart = [take(pose_first, i) - take(pose_second, i) for i in range(3)]
    force = [turn_2[i][0] * total[0] + turn_2[i][1] * total[1] + turn_2[i][2] * total[2] for i in range(3)]
    half = [[turn_1[j][0] * moment[0][m] + turn_1[j][1] * moment[1][m] + turn_1[j][2] * moment[2][m]
             for m in range(3)] for j in range(3)]
    outer = [[half[j][0] * turn_2[k][0] + half[j][1] * turn_2[k][1] + half[j][2] * turn_2[k][2]
              for k in range(3)] for j in range(3)]
    first_moment = [outer[1][2] - outer[2][1], outer[2][0] - outer[0][2], outer[0][1] - outer[1][0]]
    crossed = [apart[1] * force[2] - apart[2] * force[1], apart[2] * force[0] - apart[0] * force[2],
               apart[0] * force[1] - apart[1] * force[0]]
    second_moment = [-(crossed[i] + first_moment[i]) for i in range(3)]
    zero = jnp.zeros_like(force[0])
    loads_1 = jnp.concatenate(force + first_moment + [zero, zero], axis=0)
    loads_2 = jnp.concatenate([-value for value in force] + second_moment + [zero, zero], axis=0)
    loads_1 = jnp.concatenate(split3_rows(loads_1), axis=0).astype(BF16)
    loads_2 = jnp.concatenate(split3_rows(loads_2), axis=0).astype(BF16)
    rows = lax.broadcasted_iota(jnp.int32, (grains, pairs), 0)
    first_hot = jnp.where(rows == first[...], 1.0, 0.0).astype(BF16)
    own_hot = jnp.where(rows == row, 1.0, 0.0).astype(BF16)
    place_hot = jnp.where(rows == place, 1.0, 0.0).astype(BF16)
    near = dot(loads_1, first_hot, NT) + dot(loads_2, own_hot, NT)
    own_sum[...] = near[0:8] + near[8:16] + near[16:24]
    far = dot(loads_2, place_hot, NT)
    far = far[0:8] + far[8:16] + far[16:24]
    for index, out in enumerate((load_a, load_b, load_c, load_d)):
        out[...] = far[:, 128 * index:128 * index + 128]


def split3_rows(value):
    return [piece.astype(F32) for piece in split3(value)]


def ghost_pairs(order, first, sdf, own_results, knots, offsets, body_table, pose_pairs, payloads):
    pairs, width = knots.shape
    grains = body_table.shape[0]
    vmem = pl.BlockSpec(memory_space=pltpu.VMEM)
    smem = pl.BlockSpec(memory_space=pltpu.SMEM)
    load = jax.ShapeDtypeStruct((8, 128), F32)
    return pl.pallas_call(
        ghost_kernel,
        out_shape=[jax.ShapeDtypeStruct((8, grains), F32)] + [load] * 4,
        in_specs=[smem] * 2 + [vmem] * 15,
        out_specs=[vmem] * 5,
        scratch_shapes=[
            pltpu.VMEM((pairs, 128), F32),
            pltpu.VMEM((2, pairs * GRID, 128), F32),
        ] + pair_scratch(width, pairs),
        cost_estimate=pl.CostEstimate(flops=6 * 10**9, bytes_accessed=16 * 10**6, transcendentals=0),
        compiler_params=pltpu.CompilerParams(vmem_limit_bytes=24 * 2**20),
        name="ghost_pairs",
    )(order, first, first.reshape(1, pairs), sdf.reshape(1, pairs), own_results, knots, offsets, body_table, pose_pairs,
      *payloads)


def return_kernel(listed, own_sum, load_a, load_b, load_c, load_d, out, targets):
    signs = parity_signs()
    grains = own_sum.shape[1]
    targets[...] = jnp.zeros_like(targets)
    for base, op in ((0, "A"), (128, "B"), (256, "C"), (288, "AC"), (320, "BC"), (384, "D"), (416, "BD"), (448, "AD")):
        targets[base:base + 32, :] = one_hot_rows(listed_column(listed, signs, op), grains)
    loads = jnp.concatenate([load_a[...], load_b[...], load_c[...], load_d[...]], axis=1)
    pieces = jnp.concatenate(split3_rows(loads), axis=0).astype(BF16)
    added = dot(pieces, targets[...])
    total = own_sum[...] + (added[0:8] + added[8:16] + added[16:24])
    out[...] = total[0:6]


def return_loads(listed, own_sum, loads):
    vmem = pl.BlockSpec(memory_space=pltpu.VMEM)
    return pl.pallas_call(
        return_kernel,
        out_shape=jax.ShapeDtypeStruct((6, own_sum.shape[1]), F32),
        in_specs=[vmem] * 6,
        out_specs=vmem,
        scratch_shapes=[pltpu.VMEM((512, own_sum.shape[1]), BF16)],
        compiler_params=pltpu.CompilerParams(vmem_limit_bytes=4 * 2**20),
        name="return_loads",
    )(listed, own_sum, *loads)


def swapped(block, op, rows, cols):
    route = []
    row_step, col_step = steps_of(op)
    for r in range(rows):
        for c in range(cols):
            to_r = (r + row_step * (1 - 2 * (r % 2))) % rows
            to_c = (c + col_step * (1 - 2 * (c % 2))) % cols
            route.append((r * cols + c, to_r * cols + to_c))
    return lax.ppermute(block, ("row", "col"), route)


def local(rows, cols, sdf_grids, grain_poses, surface_nodes, send_list, pair_first, pair_sdf, pair_pose, pair_live,
          knot_cells, offsets):
    listed = send_list.reshape(8, send_list.shape[3])
    swap = lambda block, op: swapped(block, op, rows, cols)
    packed, table = pack(listed, grain_poses, sdf_grids)
    payloads = [swap(block, op) for block, op in zip(packed, OPS)]
    results, pose_pairs, order = own_pairs(
        pair_first, pair_sdf, pair_live, grain_poses, table, surface_nodes, knot_cells, offsets)
    own_sum, load_a, load_b, load_c, load_d = ghost_pairs(
        order, pair_first, pair_sdf, results, knot_cells, offsets, surface_nodes, pose_pairs, payloads)
    back_a, back_b = swap(load_a, "A"), swap(load_b, "B")
    lanes = lax.broadcasted_iota(jnp.int32, load_a.shape, 1)
    send_c = jnp.where(lanes < 32, load_c, jnp.where(lanes < 64, back_a, back_b))
    send_d = jnp.where(lanes < 32, load_d, jnp.where(lanes < 64, back_b, back_a))
    back_c, back_d = swap(send_c, "C"), swap(send_d, "D")
    return return_loads(listed, own_sum, (back_a, back_b, back_c, back_d))


def solution(mesh):
    in_specs = (
        P(("row", "col"), None),
        P(None, ("row", "col")),
        P(("row", "col"), None),
        P("row", "col", None, None),
        P(("row", "col")),
        P(("row", "col")),
        P(("row", "col")),
        P(("row", "col")),
        P(("row", "col"), None),
        P(("row", "col"), None),
    )
    out_specs = P(None, ("row", "col"))
    body = functools.partial(local, mesh.shape["row"], mesh.shape["col"])
    return jax.shard_map(body, mesh=mesh, in_specs=in_specs, out_specs=out_specs, check_vma=False)
```
